32 devices in a mesh: dp: 8 (over z, core), tensor: 4 (over y, x).
Axes of the slice: x: 2, y: 2, z: 4, core: 2. Of those that a mesh axis runs over, the one named last changes fastest.
Arguments:
- tokens: bfloat16 [8192, 2048], P('dp'), may hold values from -6 to 6
- cotangent: bfloat16 [8192, 2048], P('dp'), may hold values from -6 to 6
- seq_lengths: int32 [4], replicated, may hold values from 1536 to 2048, as said below
- slot_seq: int32 [4], replicated, may hold values from 0 to 3, each once
- w_query: float32 [2048, 2048], P('dp', 'tensor'), may hold values from -0.125 to 0.125
- w_key: float32 [2048, 2048], P('dp', 'tensor'), may hold values from -0.125 to 0.125
- w_value: float32 [2048, 2048], P('dp', 'tensor'), may hold values from -0.125 to 0.125
- b_query: float32 [2048], P('tensor'), may hold values from -3 to 3
- b_value: float32 [2048], P('tensor'), may hold values from -3 to 3
- w_out: float32 [2048, 2048], P('tensor', 'dp'), may hold values from -4 to 4
- b_out: float32 [2048], replicated, may hold values from -3 to 3
- ln1_gain: float32 [2048], replicated, may hold values from 0.5 to 1.5
- ln1_bias: float32 [2048], replicated, may hold values from -3 to 3
- w_inner: float32 [2048, 8192], P('dp', 'tensor'), may hold values from -0.125 to 0.125
- b_inner: float32 [8192], P('tensor'), may hold values from -3 to 3
- w_outer: float32 [8192, 2048], P('tensor', 'dp'), may hold values from -0.0625 to 0.0625
- b_outer: float32 [2048], replicated, may hold values from -3 to 3
- ln2_gain: float32 [2048], replicated, may hold values from 0.5 to 1.5
- ln2_bias: float32 [2048], replicated, may hold values from -3 to 3
Outputs:
- output: float32 [8192, 2048], P('dp')
- grad_tokens: float32 [8192, 2048], P('dp')
- grad_w_query: float32 [2048, 2048], P('dp', 'tensor')
- grad_w_key: float32 [2048, 2048], P('dp', 'tensor')
- grad_w_value: float32 [2048, 2048], P('dp', 'tensor')
- grad_b_query: float32 [2048], P('tensor')
- grad_b_value: float32 [2048], P('tensor')
- grad_w_out: float32 [2048, 2048], P('tensor', 'dp')
- grad_b_out: float32 [2048], replicated
- grad_ln1_gain: float32 [2048], replicated
- grad_ln1_bias: float32 [2048], replicated
- grad_w_inner: float32 [2048, 8192], P('dp', 'tensor')
- grad_b_inner: float32 [8192], P('tensor')
- grad_w_outer: float32 [8192, 2048], P('tensor', 'dp')
- grad_b_outer: float32 [2048], replicated
- grad_ln2_gain: float32 [2048], replicated
- grad_ln2_bias: float32 [2048], replicated
The draws below stay inside these ranges and needn't reach their ends.
Inputs may be any that keep to these rules, and one draw needn't show every extreme that they name: `seq_lengths`: each sequence's valid tokens; some sequence has exactly 2048 and some exactly 1536. `slot_seq`: each sequence stands in exactly one slot.
All inputs are finite; a program needn't handle non-finite values.
Results may differ from the reference program's by a relative error of at most 0.019.
Values may be sent and summed in bfloat16 or wider, within the bound.
No kernel may reach another device: no remote copies, remote signals or barrier semaphores. Data moves between devices by JAX's collectives and lax.ppermute only.
A program may use at most 256 MiB of HBM per device.

```python
import jax
import jax.numpy as jnp
from jax import lax

D = 2048
HEADS = 16
FF = 8192
HEAD_DIM = 128
SLOT = 2048
TOK_DEV = 1024
SLOTS = 4
TOKENS = 8192


def draw_seq_lengths(key, part):
    least = SLOT - TOK_DEV // 2
    drawn = jax.random.randint(key, (SLOTS,), least, SLOT + 1).astype(jnp.int32)
    return drawn.at[0].set(SLOT).at[1].set(least)


def steps_of(key, dims, shards, low, largest):
    level = 1.0
    for dim, blocks in shards:
        steps = jax.random.uniform(jax.random.fold_in(jax.random.fold_in(key, 6), dim), (blocks,), jnp.float32, low / len(shards), largest / len(shards))
        level = level * jnp.repeat(jnp.exp(steps), dims[dim] // blocks).reshape((-1,) + (1,) * (len(dims) - 1 - dim))
    return level


def noise(stream_key, shape, width, reach, cuts=(), held_as=jnp.bfloat16):
    factor_of = steps_of(stream_key, shape, cuts, -0.22, 0.18) if cuts else 1.0
    values = jax.random.normal(stream_key, shape, jnp.float32) * width * factor_of
    return jnp.minimum(jnp.maximum(values, -reach), reach).astype(held_as)


def setup_inputs(seed: int = 0) -> dict:
    keys = jax.random.split(jax.random.key(seed), 20)
    return {
        "tokens": noise(keys[0], (TOKENS, D), 1.0, 6.0, ((0, 8),)),
        "cotangent": noise(keys[1], (TOKENS, D), 1.0, 6.0, ((0, 8),)),
        "seq_lengths": draw_seq_lengths(jax.random.fold_in(keys[19], 71), 0),
        "slot_seq": jax.random.permutation(keys[3], SLOTS).astype(jnp.int32),
        "w_query": noise(keys[4], (D, D), D ** -0.5, 0.125, ((0, 8), (1, 4)), jnp.float32),
        "w_key": noise(keys[5], (D, D), D ** -0.5, 0.125, ((0, 8), (1, 4)), jnp.float32),
        "w_value": noise(keys[6], (D, D), D ** -0.5, 0.125, ((0, 8), (1, 4)), jnp.float32),
        "b_query": noise(keys[7], (D,), 0.5, 3.0, ((0, 4),), jnp.float32),
        "b_value": noise(keys[8], (D,), 0.5, 3.0, ((0, 4),), jnp.float32),
        "w_out": noise(keys[9], (D, D), (max(D // 1024, 1)) ** -0.5, 4.0, ((0, 4), (1, 8)), jnp.float32),
        "b_out": noise(keys[10], (D,), 0.5, 3.0, (), jnp.float32),
        "ln1_gain": jnp.clip(1.0 + 0.1 * jax.random.normal(keys[11], (D,), jnp.float32), 0.5, 1.5),
        "ln1_bias": noise(keys[12], (D,), 0.5, 3.0, (), jnp.float32),
        "w_inner": noise(keys[13], (D, FF), D ** -0.5, 0.125, ((0, 8), (1, 4)), jnp.float32),
        "b_inner": noise(keys[14], (FF,), 0.5, 3.0, ((0, 4),), jnp.float32),
        "w_outer": noise(keys[15], (FF, D), FF ** -0.5, 0.0625, ((0, 4), (1, 8)), jnp.float32),
        "b_outer": noise(keys[16], (D,), 0.5, 3.0, (), jnp.float32),
        "ln2_gain": jnp.clip(1.0 + 0.1 * jax.random.normal(keys[17], (D,), jnp.float32), 0.5, 1.5),
        "ln2_bias": noise(keys[18], (D,), 0.5, 3.0, (), jnp.float32),
    }


@jax.custom_vjp
def low(v):
    return lax.optimization_barrier(v.astype(jnp.bfloat16)).astype(jnp.float32)

@jax.custom_vjp
def low_back(v):
    return v

def low_keep(v):
    return (low(v), None)

def low_pass(kept, grad):
    return (grad,)

def back_keep(v):
    return (v, None)

def back_low(kept, grad):
    return (low(grad),)
low.defvjp(low_keep, low_pass)
low_back.defvjp(back_keep, back_low)
norm_eps = 1e-12

def layer_norm(resid, gain, shift):
    center = resid - lax.optimization_barrier(jnp.mean(resid, axis=-1, keepdims=True))
    spread = lax.optimization_barrier(jnp.mean(center * center, axis=-1, keepdims=True))
    return center * lax.rsqrt(spread + norm_eps) * gain + shift

def gelu_tanh(inner):
    return 0.5 * inner * (1.0 + jnp.tanh(0.7978845608 * (inner + 0.044715 * inner * inner * inner)))

def matmul_hi(left, right):
    return jnp.dot(left, right, precision=lax.Precision.HIGHEST, preferred_element_type=jnp.float32)

def slot_attention(inputs):
    query, keyed, value, live_keys = inputs
    scores = jnp.einsum('qhd,khd->hqk', query, keyed, precision=lax.Precision.HIGHEST) * HEAD_DIM ** (-0.5)
    scores = low_back(scores)
    scores = jnp.where(live_keys[None, None, :], scores, -1e+30)
    top = lax.optimization_barrier(jnp.max(scores, axis=-1, keepdims=True))
    expd = jnp.exp(scores - top)
    probs = expd / lax.optimization_barrier(jnp.sum(expd, axis=-1, keepdims=True))
    return jnp.einsum('hqk,khd->qhd', low(probs), value, precision=lax.Precision.HIGHEST)

def reference(tokens, cotangent, seq_lengths, slot_seq, w_query, w_key, w_value, b_query, b_value, w_out, b_out, ln1_gain, ln1_bias, w_inner, b_inner, w_outer, b_outer, ln2_gain, ln2_bias):
    slot_lengths = seq_lengths[slot_seq]
    key_live = jnp.arange(SLOT)[None, :] < slot_lengths[:, None]
    row_live = key_live.reshape(TOKENS).astype(jnp.float32)
    inputs = tokens.astype(jnp.float32)
    grad_out = cotangent.astype(jnp.float32) * row_live[:, None]
    shape = (SLOTS, SLOT, HEADS, HEAD_DIM)

    def forward(x, w_query, w_key, w_value, b_query, b_value, w_out, b_out, ln1_gain, ln1_bias, w_inner, b_inner, w_outer, b_outer, ln2_gain, ln2_bias):
        query = low_back(low(matmul_hi(x, low(w_query)) + b_query))
        keyed = low_back(low(matmul_hi(x, low(w_key))))
        value = low_back(low(matmul_hi(x, low(w_value)) + b_value))
        mixed = lax.map(jax.checkpoint(slot_attention), (query.reshape(shape), keyed.reshape(shape), value.reshape(shape), key_live))
        heads_out = low_back(low(mixed.reshape(TOKENS, D)))
        attn = low_back(matmul_hi(heads_out, low(w_out))) + b_out
        hidden = layer_norm(x + attn, ln1_gain, ln1_bias)
        inner = low_back(matmul_hi(low(hidden), low(w_inner)) + b_inner)
        act = low(gelu_tanh(inner))
        outer = low_back(matmul_hi(act, low(w_outer))) + b_outer
        return layer_norm(hidden + outer, ln2_gain, ln2_bias)
    output, pull = jax.vjp(forward, inputs, w_query, w_key, w_value, b_query, b_value, w_out, b_out, ln1_gain, ln1_bias, w_inner, b_inner, w_outer, b_outer, ln2_gain, ln2_bias)
    grads = pull(grad_out)
    return (output, grads[0], grads[1], grads[2], grads[3], grads[4], grads[5], grads[6], grads[7], grads[8], grads[9], grads[10], grads[11], grads[12], grads[13], grads[14], grads[15])
```

```python
import functools

import jax
import jax.numpy as jnp
from jax import lax
from jax.experimental import pallas as pl
from jax.experimental.pallas import tpu as pltpu
from jax.sharding import PartitionSpec as P

HEAD_DIM = 128
SLOT = 2048
LOG2E = 1.4426950408889634

norm_eps = 1e-12

F32 = jnp.float32
LOW = jnp.bfloat16
BOTH_LAST = (((1,), (1,)), ((), ()))
BOTH_FIRST = (((0,), (0,)), ((), ()))


def layer_norm(resid, gain, shift):
    center = resid - jnp.mean(resid, axis=-1, keepdims=True)
    spread = jnp.mean(center * center, axis=-1, keepdims=True)
    return center * lax.rsqrt(spread + norm_eps) * gain + shift


def gelu_tanh(inner):
    return 0.5 * inner * (1.0 + jnp.tanh(0.7978845608 * (inner + 0.044715 * inner * inner * inner)))


def mat_bf(left, right):
    return jnp.dot(left, right, preferred_element_type=F32)


def mat_last(left, right):
    return lax.dot_general(left, right, BOTH_LAST, preferred_element_type=F32)


def mat_first(left, right):
    return lax.dot_general(left, right, BOTH_FIRST, preferred_element_type=F32)


def swap(value, axis, flip):
    count = lax.axis_size(axis)
    return lax.ppermute(value, axis, [(source, source ^ flip) for source in range(count)])


def after(value, *others):
    return lax.optimization_barrier((value, *others))[0]


def gather_rows(block):
    half = block.shape[0] // 2
    one, two = swap(block, "tensor", 1), swap(block, "tensor", 2)
    three_top = swap(two[:half], "tensor", 1)
    three_low = swap(one[half:], "tensor", 2)
    rows = [block, one, two, three_top, three_low]
    count, flip = lax.axis_size("tensor"), 4
    while flip < count:
        rows.append(swap(jnp.concatenate(rows), "tensor", flip))
        flip *= 2
    return jnp.concatenate(rows)


def scatter_rows(part, rows):
    count = lax.axis_size("tensor")
    block = rows // count
    half = block // 2
    flip = count // 2
    extra = None
    while flip >= 4:
        away = part(flip * block, 2 * flip * block)
        if extra is not None:
            away = away + extra[flip * block :].astype(F32)
        come = swap(away.astype(LOW), "tensor", flip)
        extra = come if extra is None else extra[: flip * block].astype(F32) + come.astype(F32)
        flip //= 2

    def piece(k):
        value = part(k * block, (k + 1) * block)
        if extra is not None:
            value = value + extra[k * block : (k + 1) * block].astype(F32)
        return value

    three = piece(3).astype(LOW)
    come_top = swap(three[:half], "tensor", 1)
    come_low = swap(three[half:], "tensor", 2)
    one, two = piece(1), piece(2)
    one = jnp.concatenate([one[:half].astype(LOW), (one[half:] + come_low.astype(F32)).astype(LOW)])
    two = jnp.concatenate([(two[:half] + come_top.astype(F32)).astype(LOW), two[half:].astype(LOW)])
    come_one, come_two = swap(one, "tensor", 1), swap(two, "tensor", 2)
    return piece(0) + come_one.astype(F32) + come_two.astype(F32)


def fwd_kernel(q_ref,ko_ref,kf_ref,vo_ref,vf_ref,bo_ref,bf_ref,o_ref,l_ref,*,scale):
    q=q_ref[...]
    so=lax.dot_general(q,ko_ref[...],BOTH_LAST,preferred_element_type=F32)*scale+bo_ref[...]
    sf=lax.dot_general(q,kf_ref[...],BOTH_LAST,preferred_element_type=F32)*scale+bf_ref[...]
    top=jnp.maximum(jnp.max(so,axis=1,keepdims=True),jnp.max(sf,axis=1,keepdims=True))
    po=jnp.exp2(so-top); pf=jnp.exp2(sf-top)
    tot=jnp.sum(po,axis=1,keepdims=True)+jnp.sum(pf,axis=1,keepdims=True)
    o=jnp.dot(po.astype(LOW),vo_ref[...],preferred_element_type=F32)+jnp.dot(pf.astype(LOW),vf_ref[...],preferred_element_type=F32)
    o_ref[...]=(o/tot).astype(LOW)
    lse=top+jnp.log2(tot)
    l_ref[0]=jnp.transpose(jnp.broadcast_to(lse,(lse.shape[0],HEAD_DIM)))[0:1,:]
def attn_fwd(qkv,kv_far,bias_own,bias_far,heads,bq=256):
    rows=qkv.shape[0]
    scale=LOG2E*HEAD_DIM**-0.5
    return pl.pallas_call(
        functools.partial(fwd_kernel,scale=scale),
        grid=(heads,rows//bq),
        in_specs=[pl.BlockSpec((bq,HEAD_DIM),lambda h,i:(i,h)),
          pl.BlockSpec((rows,HEAD_DIM),lambda h,i:(0,heads+h)),
          pl.BlockSpec((rows,HEAD_DIM),lambda h,i:(0,h)),
          pl.BlockSpec((rows,HEAD_DIM),lambda h,i:(0,2*heads+h)),
          pl.BlockSpec((rows,HEAD_DIM),lambda h,i:(0,heads+h)),
          pl.BlockSpec((1,rows),lambda h,i:(0,0)),
          pl.BlockSpec((1,rows),lambda h,i:(0,0))],
        out_specs=[pl.BlockSpec((bq,HEAD_DIM),lambda h,i:(i,h)),pl.BlockSpec((1,1,bq),lambda h,i:(h,0,i))],
        out_shape=[jax.ShapeDtypeStruct((rows,heads*HEAD_DIM),LOW),jax.ShapeDtypeStruct((heads,1,rows),F32)],
        compiler_params=pltpu.CompilerParams(vmem_limit_bytes=48<<20),
        cost_estimate=pl.CostEstimate(flops=4*rows*2*rows*HEAD_DIM*heads,transcendentals=heads*rows*2*rows,bytes_accessed=heads*HEAD_DIM*rows*2*6),
        name='attention_forward')(qkv,qkv,kv_far,qkv,kv_far,bias_own,bias_far)

def bwd_kernel(q_ref,do_ref,o_ref,l_ref,ko_ref,kf_ref,vo_ref,vf_ref,bo_ref,bf_ref,dq_ref,dko_ref,dvo_ref,dkf_ref,dvf_ref,
               ako,avo,akf,avf,kto,ktf,*,scale,chunk):
    i=pl.program_id(1); last=pl.num_programs(1)-1
    @pl.when(i==0)
    def _():
        kto[...]=jnp.transpose(ko_ref[...]); ktf[...]=jnp.transpose(kf_ref[...])
        for a in (ako,avo,akf,avf): a[...]=jnp.zeros_like(a)
    q=q_ref[...]; do=do_ref[...]
    lse=l_ref[0]
    delta=jnp.sum(jnp.transpose(do.astype(F32)*o_ref[...].astype(F32)),axis=0,keepdims=True)
    rows=ko_ref.shape[0]; bq=q.shape[0]
    dqt=jnp.zeros((HEAD_DIM,bq),F32)
    for k_ref,v_ref,b_ref,ak,av,kt in ((ko_ref,vo_ref,bo_ref,ako,avo,kto),(kf_ref,vf_ref,bf_ref,akf,avf,ktf)):
        for c in range(rows//chunk):
            sl=pl.ds(c*chunk,chunk)
            st=lax.dot_general(k_ref[sl,:],q,BOTH_LAST,preferred_element_type=F32)
            b=b_ref[sl,:]
            b=jnp.concatenate([b]*(bq//HEAD_DIM),axis=1)
            p=jnp.exp2(st*scale+b-lse)
            dp=lax.dot_general(v_ref[sl,:],do,BOTH_LAST,preferred_element_type=F32)
            ds=(p*(dp-delta)).astype(LOW)
            av[sl,:]+=jnp.dot(p.astype(LOW),do,preferred_element_type=F32)
            ak[sl,:]+=jnp.dot(ds,q,preferred_element_type=F32)
            dqt=dqt+jnp.dot(kt[:,sl],ds,preferred_element_type=F32)
    s=HEAD_DIM**-0.5
    dq_ref[...]=(jnp.transpose(dqt)*s).astype(LOW)
    @pl.when(i==last)
    def _():
        dko_ref[...]=ako[...]*s; dvo_ref[...]=avo[...]
        dkf_ref[...]=(akf[...]*s).astype(LOW); dvf_ref[...]=avf[...].astype(LOW)
def attn_bwd(qkv,kv_far,do,o,lse,bias_own,bias_far,heads,bq=256,chunk=512):
    rows=qkv.shape[0]
    scale=LOG2E*HEAD_DIM**-0.5
    full=lambda off: pl.BlockSpec((rows,HEAD_DIM),lambda h,i:(0,off+h))
    qb=pl.BlockSpec((bq,HEAD_DIM),lambda h,i:(i,h))
    return pl.pallas_call(
        functools.partial(bwd_kernel,scale=scale,chunk=chunk),
        grid=(heads,rows//bq),
        in_specs=[qb,qb,qb,pl.BlockSpec((1,1,bq),lambda h,i:(h,0,i)),
          full(heads),full(0),full(2*heads),full(heads),
          pl.BlockSpec((rows,HEAD_DIM),lambda h,i:(0,0)),pl.BlockSpec((rows,HEAD_DIM),lambda h,i:(0,0))],
        out_specs=[qb,full(0),full(0),full(0),full(0)],
        out_shape=[jax.ShapeDtypeStruct((rows,heads*HEAD_DIM),LOW)]+[jax.ShapeDtypeStruct((rows,heads*HEAD_DIM),F32)]*2+[jax.ShapeDtypeStruct((rows,heads*HEAD_DIM),LOW)]*2,
        scratch_shapes=[pltpu.VMEM((rows,HEAD_DIM),F32)]*4+[pltpu.VMEM((HEAD_DIM,rows),LOW)]*2,
        compiler_params=pltpu.CompilerParams(vmem_limit_bytes=48<<20),
        cost_estimate=pl.CostEstimate(flops=10*rows*2*rows*HEAD_DIM*heads,transcendentals=heads*rows*2*rows,bytes_accessed=heads*HEAD_DIM*rows*2*12),
        name='attention_backward')(qkv,do,o,lse,qkv,kv_far,qkv,kv_far,bias_own,bias_far)


def on_device(
    tokens,
    cotangent,
    seq_lengths,
    slot_seq,
    w_query,
    w_key,
    w_value,
    b_query,
    b_value,
    w_out,
    b_out,
    ln1_gain,
    ln1_bias,
    w_inner,
    b_inner,
    w_outer,
    b_outer,
    ln2_gain,
    ln2_bias,
):
    tok_rows, model = tokens.shape
    assert SLOT == 2 * tok_rows
    tensor_count = lax.axis_size("tensor")
    tensor_place = lax.axis_index("tensor")
    block = tok_rows // tensor_count
    width_here = w_query.shape[1]
    heads_here = width_here // HEAD_DIM
    dp_place = lax.axis_index("dp")
    my_slot = dp_place // 2
    my_spot = dp_place % 2
    slot_ids = jnp.arange(slot_seq.shape[0])
    slot_lengths = jnp.sum(
        jnp.where(slot_seq[:, None] == slot_ids[None, :], seq_lengths[None, :], 0), axis=1
    )
    my_length = jnp.sum(jnp.where(slot_ids == my_slot, slot_lengths, 0))
    row_ids = jnp.arange(tok_rows)
    place = ((row_ids // block) ^ tensor_place) * block + row_ids % block
    own_bias = jnp.where(my_spot * tok_rows + place < my_length, 0.0, -1e30).astype(F32)
    far_bias = jnp.where((1 - my_spot) * tok_rows + place < my_length, 0.0, -1e30).astype(F32)
    own_bias_wide = jnp.broadcast_to(own_bias[:, None], (tok_rows, HEAD_DIM))
    far_bias_wide = jnp.broadcast_to(far_bias[:, None], (tok_rows, HEAD_DIM))

    def my_block(value):
        return lax.dynamic_slice_in_dim(value, tensor_place * block, block, 0)

    def reorder(value):
        return jnp.concatenate(
            [
                lax.dynamic_slice_in_dim(value, (tensor_place ^ k) * block, block, 0)
                for k in range(tensor_count)
            ]
        )

    row_live = (my_spot * tok_rows + place[:block] < my_length).astype(F32)
    rows_in = reorder(tokens)
    in_here = my_block(tokens).astype(F32)
    grad_out = my_block(cotangent).astype(F32) * row_live[:, None]

    low_qkv = jnp.concatenate([w_query, w_key, w_value], axis=1).astype(LOW)
    low_out = w_out.T.astype(LOW)
    low_inner = w_inner.astype(LOW)
    low_outer = w_outer.T.astype(LOW)
    full_qkv = lax.all_gather(low_qkv, "dp", axis=0, tiled=True)
    full_out = lax.all_gather(low_out, "dp", axis=0, tiled=True)
    full_inner = lax.all_gather(low_inner, "dp", axis=0, tiled=True)
    full_outer = lax.all_gather(low_outer, "dp", axis=0, tiled=True)

    b_qkv = jnp.concatenate([b_query, jnp.zeros_like(b_query), b_value])
    qkv = (mat_bf(rows_in, full_qkv) + b_qkv).astype(LOW)
    far_kv = swap(qkv[:, width_here:], "dp", 1)
    mixed, lse = attn_fwd(qkv, far_kv, own_bias[None], far_bias[None], heads_here)

    attn = scatter_rows(lambda a, b: mat_last(mixed[a:b], full_out), tok_rows)
    hidden, norm_one_back = jax.vjp(layer_norm, in_here + (attn + b_out), ln1_gain, ln1_bias)
    hidden_low = gather_rows(hidden.astype(LOW))
    inner = mat_bf(hidden_low, full_inner) + b_inner
    act_low = gelu_tanh(inner).astype(LOW)
    outer = scatter_rows(lambda a, b: mat_last(act_low[a:b], full_outer), tok_rows)
    output, norm_two_back = jax.vjp(layer_norm, hidden + (outer + b_outer), ln2_gain, ln2_bias)
    grad_two, grad_ln2_gain, grad_ln2_bias = norm_two_back(grad_out)
    grad_b_outer = jnp.sum(grad_two, axis=0)
    outer_low = gather_rows(grad_two.astype(LOW))
    output = reorder(gather_rows(after(output.astype(LOW), outer_low))).astype(F32)

    grad_w_outer = lax.psum_scatter(
        mat_first(outer_low, act_low).astype(LOW), "dp", scatter_dimension=0, tiled=True
    )
    grad_act = mat_bf(outer_low, full_outer)
    gelu_value, gelu_back = jax.vjp(gelu_tanh, inner)
    inner_low = gelu_back(grad_act)[0].astype(LOW)
    grad_b_inner = jnp.sum(inner_low.astype(F32), axis=0)
    grad_hidden = grad_two + scatter_rows(lambda a, b: mat_last(inner_low[a:b], full_inner), tok_rows)
    grad_w_inner = lax.psum_scatter(
        mat_first(hidden_low, inner_low).astype(LOW), "dp", scatter_dimension=0, tiled=True
    )
    grad_one, grad_ln1_gain, grad_ln1_bias = norm_one_back(grad_hidden)
    grad_b_out = jnp.sum(grad_one, axis=0)
    attn_low = gather_rows(grad_one.astype(LOW))
    mixed_low = mat_bf(attn_low, full_out).astype(LOW)
    grad_w_out = lax.psum_scatter(
        mat_first(attn_low, mixed).astype(LOW), "dp", scatter_dimension=0, tiled=True
    )
    query_low, own_key, own_value, far_key, far_value = attn_bwd(
        qkv, far_kv, mixed_low, mixed, lse, own_bias_wide, far_bias_wide, heads_here
    )
    key_low = (own_key + swap(far_key, "dp", 1).astype(F32)).astype(LOW)
    value_low = (own_value + swap(far_value, "dp", 1).astype(F32)).astype(LOW)
    qkv_low = jnp.concatenate([query_low, key_low, value_low], axis=1)
    grad_w_qkv = lax.psum_scatter(
        mat_first(rows_in, qkv_low).astype(LOW), "dp", scatter_dimension=0, tiled=True
    )
    grad_b_qkv = jnp.sum(qkv_low.astype(F32), axis=0)
    input_part = scatter_rows(lambda a, b: mat_last(qkv_low[a:b], full_qkv), tok_rows)
    grad_tokens = reorder(gather_rows((grad_one + input_part).astype(LOW))).astype(F32)

    over_rows = lax.psum(
        jnp.stack(
            [grad_b_out, grad_b_outer, grad_ln1_gain, grad_ln1_bias, grad_ln2_gain, grad_ln2_bias]
        ),
        ("dp", "tensor"),
    )
    grad_b_inner, grad_b_qkv = lax.psum((grad_b_inner, grad_b_qkv), "dp")
    grad_b_out, grad_b_outer, grad_ln1_gain, grad_ln1_bias, grad_ln2_gain, grad_ln2_bias = over_rows
    grad_w_query, grad_w_key, grad_w_value = jnp.split(grad_w_qkv.astype(F32), 3, axis=1)
    return (
        output,
        grad_tokens,
        grad_w_query,
        grad_w_key,
        grad_w_value,
        grad_b_qkv[:width_here],
        grad_b_qkv[2 * width_here :],
        grad_w_out.T.astype(F32),
        grad_b_out,
        grad_ln1_gain,
        grad_ln1_bias,
        grad_w_inner.astype(F32),
        grad_b_inner,
        grad_w_outer.T.astype(F32),
        grad_b_outer,
        grad_ln2_gain,
        grad_ln2_bias,
    )


def solution(mesh):
    return jax.shard_map(
        on_device,
        mesh=mesh,
        in_specs=(
            P("dp", None),
            P("dp", None),
            P(),
            P(),
            P("dp", "tensor"),
            P("dp", "tensor"),
            P("dp", "tensor"),
            P("tensor"),
            P("tensor"),
            P("tensor", "dp"),
            P(),
            P(),
            P(),
            P("dp", "tensor"),
            P("tensor"),
            P("tensor", "dp"),
            P(),
            P(),
            P(),
        ),
        out_specs=(
            P("dp", None),
            P("dp", None),
            P("dp", "tensor"),
            P("dp", "tensor"),
            P("dp", "tensor"),
            P("tensor"),
            P("tensor"),
            P("tensor", "dp"),
            P(),
            P(),
            P(),
            P("dp", "tensor"),
            P("tensor"),
            P("tensor", "dp"),
            P(),
            P(),
            P(),
        ),
        check_vma=False,
    )
```

```python
import functools

import jax
import jax.numpy as jnp
from jax import lax
from jax.experimental import pallas as pl
from jax.experimental.pallas import tpu as pltpu
from jax.sharding import PartitionSpec as P

HEAD_DIM = 128
SLOT = 2048
LOG2E = 1.4426950408889634

norm_eps = 1e-12

F32 = jnp.float32
LOW = jnp.bfloat16
BOTH_LAST = (((1,), (1,)), ((), ()))
BOTH_FIRST = (((0,), (0,)), ((), ()))


def layer_norm(resid, gain, shift):
    center = resid - jnp.mean(resid, axis=-1, keepdims=True)
    spread = jnp.mean(center * center, axis=-1, keepdims=True)
    return center * lax.rsqrt(spread + norm_eps) * gain + shift


def gelu_tanh(inner):
    return 0.5 * inner * (1.0 + jnp.tanh(0.7978845608 * (inner + 0.044715 * inner * inner * inner)))


def mat_bf(left, right):
    return jnp.dot(left, right, preferred_element_type=F32)


def mat_last(left, right):
    return lax.dot_general(left, right, BOTH_LAST, preferred_element_type=F32)


def mat_first(left, right):
    return lax.dot_general(left, right, BOTH_FIRST, preferred_element_type=F32)


def swap(value, axis, flip):
    count = lax.axis_size(axis)
    return lax.ppermute(value, axis, [(source, source ^ flip) for source in range(count)])


def after(value, *others):
    return lax.optimization_barrier((value, *others))[0]


def everyone(value, axes):
    for axis in axes:
        flip = 1
        while flip < lax.axis_size(axis):
            value = value + swap(value, axis, flip)
            flip *= 2
    return value


def gather_rows(block):
    half = block.shape[0] // 2
    one, two = swap(block, "tensor", 1), swap(block, "tensor", 2)
    three_top = swap(two[:half], "tensor", 1)
    three_low = swap(one[half:], "tensor", 2)
    rows = [block, one, two, three_top, three_low]
    count, flip = lax.axis_size("tensor"), 4
    while flip < count:
        rows.append(swap(jnp.concatenate(rows), "tensor", flip))
        flip *= 2
    return jnp.concatenate(rows)


def scatter_rows(part, rows):
    count = lax.axis_size("tensor")
    block = rows // count
    half = block // 2
    flip = count // 2
    extra = None
    while flip >= 4:
        away = part(flip * block, 2 * flip * block)
        if extra is not None:
            away = away + extra[flip * block :].astype(F32)
        come = swap(away.astype(LOW), "tensor", flip)
        extra = come if extra is None else extra[: flip * block].astype(F32) + come.astype(F32)
        flip //= 2

    def piece(k):
        value = part(k * block, (k + 1) * block)
        if extra is not None:
            value = value + extra[k * block : (k + 1) * block].astype(F32)
        return value

    three = piece(3).astype(LOW)
    come_top = swap(three[:half], "tensor", 1)
    come_low = swap(three[half:], "tensor", 2)
    one, two = piece(1), piece(2)
    one = jnp.concatenate([one[:half].astype(LOW), (one[half:] + come_low.astype(F32)).astype(LOW)])
    two = jnp.concatenate([(two[:half] + come_top.astype(F32)).astype(LOW), two[half:].astype(LOW)])
    come_one, come_two = swap(one, "tensor", 1), swap(two, "tensor", 2)
    return piece(0) + come_one.astype(F32) + come_two.astype(F32)


def fwd_kernel(q_ref,ko_ref,kf_ref,vo_ref,vf_ref,bo_ref,bf_ref,o_ref,l_ref,*,scale):
    q=q_ref[...]
    so=lax.dot_general(q,ko_ref[...],BOTH_LAST,preferred_element_type=F32)*scale+bo_ref[...]
    sf=lax.dot_general(q,kf_ref[...],BOTH_LAST,preferred_element_type=F32)*scale+bf_ref[...]
    top=jnp.maximum(jnp.max(so,axis=1,keepdims=True),jnp.max(sf,axis=1,keepdims=True))
    po=jnp.exp2(so-top); pf=jnp.exp2(sf-top)
    tot=jnp.sum(po,axis=1,keepdims=True)+jnp.sum(pf,axis=1,keepdims=True)
    o=jnp.dot(po.astype(LOW),vo_ref[...],preferred_element_type=F32)+jnp.dot(pf.astype(LOW),vf_ref[...],preferred_element_type=F32)
    o_ref[...]=(o/tot).astype(LOW)
    lse=top+jnp.log2(tot)
    l_ref[0]=jnp.transpose(jnp.broadcast_to(lse,(lse.shape[0],HEAD_DIM)))[0:1,:]
def attn_fwd(qkv,kv_far,bias_own,bias_far,heads,bq=256):
    rows=qkv.shape[0]
    scale=LOG2E*HEAD_DIM**-0.5
    return pl.pallas_call(
        functools.partial(fwd_kernel,scale=scale),
        grid=(heads,rows//bq),
        in_specs=[pl.BlockSpec((bq,HEAD_DIM),lambda h,i:(i,h)),
          pl.BlockSpec((rows,HEAD_DIM),lambda h,i:(0,heads+h)),
          pl.BlockSpec((rows,HEAD_DIM),lambda h,i:(0,h)),
          pl.BlockSpec((rows,HEAD_DIM),lambda h,i:(0,2*heads+h)),
          pl.BlockSpec((rows,HEAD_DIM),lambda h,i:(0,heads+h)),
          pl.BlockSpec((1,rows),lambda h,i:(0,0)),
          pl.BlockSpec((1,rows),lambda h,i:(0,0))],
        out_specs=[pl.BlockSpec((bq,HEAD_DIM),lambda h,i:(i,h)),pl.BlockSpec((1,1,bq),lambda h,i:(h,0,i))],
        out_shape=[jax.ShapeDtypeStruct((rows,heads*HEAD_DIM),LOW),jax.ShapeDtypeStruct((heads,1,rows),F32)],
        compiler_params=pltpu.CompilerParams(vmem_limit_bytes=48<<20),
        cost_estimate=pl.CostEstimate(flops=4*rows*2*rows*HEAD_DIM*heads,transcendentals=heads*rows*2*rows,bytes_accessed=heads*HEAD_DIM*rows*2*6),
        name='attention_forward')(qkv,qkv,kv_far,qkv,kv_far,bias_own,bias_far)

def bwd_kernel(q_ref,do_ref,o_ref,l_ref,ko_ref,kf_ref,vo_ref,vf_ref,bo_ref,bf_ref,dq_ref,dko_ref,dvo_ref,dkf_ref,dvf_ref,
               ako,avo,akf,avf,kto,ktf,*,scale,chunk):
    i=pl.program_id(1); last=pl.num_programs(1)-1
    @pl.when(i==0)
    def _():
        kto[...]=jnp.transpose(ko_ref[...]); ktf[...]=jnp.transpose(kf_ref[...])
        for a in (ako,avo,akf,avf): a[...]=jnp.zeros_like(a)
    q=q_ref[...]; do=do_ref[...]
    lse=l_ref[0]
    delta=jnp.sum(jnp.transpose(do.astype(F32)*o_ref[...].astype(F32)),axis=0,keepdims=True)
    rows=ko_ref.shape[0]; bq=q.shape[0]
    dqt=jnp.zeros((HEAD_DIM,bq),F32)
    for k_ref,v_ref,b_ref,ak,av,kt in ((ko_ref,vo_ref,bo_ref,ako,avo,kto),(kf_ref,vf_ref,bf_ref,akf,avf,ktf)):
        for c in range(rows//chunk):
            sl=pl.ds(c*chunk,chunk)
            st=lax.dot_general(k_ref[sl,:],q,BOTH_LAST,preferred_element_type=F32)
            b=b_ref[sl,:]
            b=jnp.concatenate([b]*(bq//HEAD_DIM),axis=1)
            p=jnp.exp2(st*scale+b-lse)
            dp=lax.dot_general(v_ref[sl,:],do,BOTH_LAST,preferred_element_type=F32)
            ds=(p*(dp-delta)).astype(LOW)
            av[sl,:]+=jnp.dot(p.astype(LOW),do,preferred_element_type=F32)
            ak[sl,:]+=jnp.dot(ds,q,preferred_element_type=F32)
            dqt=dqt+jnp.dot(kt[:,sl],ds,preferred_element_type=F32)
    s=HEAD_DIM**-0.5
    dq_ref[...]=(jnp.transpose(dqt)*s).astype(LOW)
    @pl.when(i==last)
    def _():
        dko_ref[...]=ako[...]*s; dvo_ref[...]=avo[...]
        dkf_ref[...]=(akf[...]*s).astype(LOW); dvf_ref[...]=avf[...].astype(LOW)
def attn_bwd(qkv,kv_far,do,o,lse,bias_own,bias_far,heads,bq=256,chunk=512):
    rows=qkv.shape[0]
    scale=LOG2E*HEAD_DIM**-0.5
    full=lambda off: pl.BlockSpec((rows,HEAD_DIM),lambda h,i:(0,off+h))
    qb=pl.BlockSpec((bq,HEAD_DIM),lambda h,i:(i,h))
    return pl.pallas_call(
        functools.partial(bwd_kernel,scale=scale,chunk=chunk),
        grid=(heads,rows//bq),
        in_specs=[qb,qb,qb,pl.BlockSpec((1,1,bq),lambda h,i:(h,0,i)),
          full(heads),full(0),full(2*heads),full(heads),
          pl.BlockSpec((rows,HEAD_DIM),lambda h,i:(0,0)),pl.BlockSpec((rows,HEAD_DIM),lambda h,i:(0,0))],
        out_specs=[qb,full(0),full(0),full(0),full(0)],
        out_shape=[jax.ShapeDtypeStruct((rows,heads*HEAD_DIM),LOW)]+[jax.ShapeDtypeStruct((rows,heads*HEAD_DIM),F32)]*2+[jax.ShapeDtypeStruct((rows,heads*HEAD_DIM),LOW)]*2,
        scratch_shapes=[pltpu.VMEM((rows,HEAD_DIM),F32)]*4+[pltpu.VMEM((HEAD_DIM,rows),LOW)]*2,
        compiler_params=pltpu.CompilerParams(vmem_limit_bytes=48<<20),
        cost_estimate=pl.CostEstimate(flops=10*rows*2*rows*HEAD_DIM*heads,transcendentals=heads*rows*2*rows,bytes_accessed=heads*HEAD_DIM*rows*2*12),
        name='attention_backward')(qkv,do,o,lse,qkv,kv_far,qkv,kv_far,bias_own,bias_far)


def on_device(
    tokens,
    cotangent,
    seq_lengths,
    slot_seq,
    w_query,
    w_key,
    w_value,
    b_query,
    b_value,
    w_out,
    b_out,
    ln1_gain,
    ln1_bias,
    w_inner,
    b_inner,
    w_outer,
    b_outer,
    ln2_gain,
    ln2_bias,
):
    tok_rows, model = tokens.shape
    assert SLOT == 2 * tok_rows
    tensor_count = lax.axis_size("tensor")
    tensor_place = lax.axis_index("tensor")
    block = tok_rows // tensor_count
    width_here = w_query.shape[1]
    heads_here = width_here // HEAD_DIM
    dp_place = lax.axis_index("dp")
    my_slot = dp_place // 2
    my_spot = dp_place % 2
    slot_ids = jnp.arange(slot_seq.shape[0])
    slot_lengths = jnp.sum(
        jnp.where(slot_seq[:, None] == slot_ids[None, :], seq_lengths[None, :], 0), axis=1
    )
    my_length = jnp.sum(jnp.where(slot_ids == my_slot, slot_lengths, 0))
    row_ids = jnp.arange(tok_rows)
    place = ((row_ids // block) ^ tensor_place) * block + row_ids % block
    own_bias = jnp.where(my_spot * tok_rows + place < my_length, 0.0, -1e30).astype(F32)
    far_bias = jnp.where((1 - my_spot) * tok_rows + place < my_length, 0.0, -1e30).astype(F32)
    own_bias_wide = jnp.broadcast_to(own_bias[:, None], (tok_rows, HEAD_DIM))
    far_bias_wide = jnp.broadcast_to(far_bias[:, None], (tok_rows, HEAD_DIM))

    def my_block(value):
        return lax.dynamic_slice_in_dim(value, tensor_place * block, block, 0)

    def reorder(value):
        return jnp.concatenate(
            [
                lax.dynamic_slice_in_dim(value, (tensor_place ^ k) * block, block, 0)
                for k in range(tensor_count)
            ]
        )

    row_live = (my_spot * tok_rows + place[:block] < my_length).astype(F32)
    rows_in = reorder(tokens)
    in_here = my_block(tokens).astype(F32)
    grad_out = my_block(cotangent).astype(F32) * row_live[:, None]

    low_attn = jnp.concatenate([w_query, w_key, w_value, w_out.T], axis=1).astype(LOW)
    low_inner = w_inner.astype(LOW)
    low_outer = w_outer.T.astype(LOW)
    full_attn = lax.all_gather(low_attn, "dp", axis=0, tiled=True)
    full_qkv, full_out = full_attn[:, : 3 * width_here], full_attn[:, 3 * width_here :]
    full_inner = lax.all_gather(low_inner, "dp", axis=0, tiled=True)
    full_outer = lax.all_gather(low_outer, "dp", axis=0, tiled=True)

    b_qkv = jnp.concatenate([b_query, jnp.zeros_like(b_query), b_value])
    qkv = (mat_bf(rows_in, full_qkv) + b_qkv).astype(LOW)
    far_kv = swap(qkv[:, width_here:], "dp", 1)
    mixed, lse = attn_fwd(qkv, far_kv, own_bias[None], far_bias[None], heads_here)

    attn = scatter_rows(lambda a, b: mat_last(mixed[a:b], full_out), tok_rows)
    hidden, norm_one_back = jax.vjp(layer_norm, in_here + (attn + b_out), ln1_gain, ln1_bias)
    hidden_low = gather_rows(hidden.astype(LOW))
    inner = mat_bf(hidden_low, full_inner) + b_inner
    act_low = gelu_tanh(inner).astype(LOW)
    outer = scatter_rows(lambda a, b: mat_last(act_low[a:b], full_outer), tok_rows)
    output, norm_two_back = jax.vjp(layer_norm, hidden + (outer + b_outer), ln2_gain, ln2_bias)
    grad_two, grad_ln2_gain, grad_ln2_bias = norm_two_back(grad_out)
    grad_b_outer = jnp.sum(grad_two, axis=0)
    outer_low = gather_rows(grad_two.astype(LOW))
    output = reorder(gather_rows(after(output.astype(LOW), outer_low))).astype(F32)

    grad_w_outer = mat_first(outer_low, act_low).astype(LOW)
    grad_act = mat_bf(after(outer_low, grad_w_outer), full_outer)
    gelu_value, gelu_back = jax.vjp(gelu_tanh, inner)
    inner_low = gelu_back(grad_act)[0].astype(LOW)
    grad_b_inner = jnp.sum(inner_low.astype(F32), axis=0)
    grad_hidden = grad_two + scatter_rows(lambda a, b: mat_last(inner_low[a:b], full_inner), tok_rows)
    grad_w_inner = mat_first(hidden_low, inner_low).astype(LOW)
    grad_hidden = after(grad_hidden, grad_w_inner)
    grad_one, grad_ln1_gain, grad_ln1_bias = norm_one_back(grad_hidden)
    grad_b_out = jnp.sum(grad_one, axis=0)
    attn_low = gather_rows(grad_one.astype(LOW))
    mixed_low = mat_bf(attn_low, full_out).astype(LOW)
    grad_w_out = mat_first(attn_low, mixed).astype(LOW)
    query_low, own_key, own_value, far_key, far_value = attn_bwd(
        qkv, far_kv, mixed_low, mixed, lse, own_bias_wide, far_bias_wide, heads_here
    )
    key_low = (own_key + swap(far_key, "dp", 1).astype(F32)).astype(LOW)
    value_low = (own_value + swap(far_value, "dp", 1).astype(F32)).astype(LOW)
    qkv_low = jnp.concatenate([query_low, key_low, value_low], axis=1)
    grad_w_qkv = mat_first(rows_in, qkv_low).astype(LOW)
    grad_w_attn = jnp.concatenate([grad_w_qkv, grad_w_out], axis=1)
    grad_w_outer, grad_w_inner, grad_w_attn = (
        lax.psum_scatter(grad, "dp", scatter_dimension=0, tiled=True).astype(F32)
        for grad in (grad_w_outer, grad_w_inner, grad_w_attn)
    )
    grad_b_qkv = jnp.sum(qkv_low.astype(F32), axis=0)
    input_part = scatter_rows(lambda a, b: mat_last(qkv_low[a:b], full_qkv), tok_rows)
    grad_tokens = reorder(gather_rows((grad_one + input_part).astype(LOW))).astype(F32)

    over_rows = everyone(
        jnp.stack(
            [grad_b_out, grad_b_outer, grad_ln1_gain, grad_ln1_bias, grad_ln2_gain, grad_ln2_bias]
        ),
        ("tensor", "dp"),
    )
    grad_b_inner = everyone(grad_b_inner, ("dp",))
    grad_b_qkv = everyone(grad_b_qkv, ("dp",))
    grad_b_out, grad_b_outer, grad_ln1_gain, grad_ln1_bias, grad_ln2_gain, grad_ln2_bias = over_rows
    grad_w_query, grad_w_key, grad_w_value, grad_w_out = jnp.split(grad_w_attn, 4, axis=1)
    return (
        output,
        grad_tokens,
        grad_w_query,
        grad_w_key,
        grad_w_value,
        grad_b_qkv[:width_here],
        grad_b_qkv[2 * width_here :],
        grad_w_out.T,
        grad_b_out,
        grad_ln1_gain,
        grad_ln1_bias,
        grad_w_inner,
        grad_b_inner,
        grad_w_outer.T,
        grad_b_outer,
        grad_ln2_gain,
        grad_ln2_bias,
    )


def solution(mesh):
    return jax.shard_map(
        on_device,
        mesh=mesh,
        in_specs=(
            P("dp", None),
            P("dp", None),
            P(),
            P(),
            P("dp", "tensor"),
            P("dp", "tensor"),
            P("dp", "tensor"),
            P("tensor"),
            P("tensor"),
            P("tensor", "dp"),
            P(),
            P(),
            P(),
            P("dp", "tensor"),
            P("tensor"),
            P("tensor", "dp"),
            P(),
            P(),
            P(),
        ),
        out_specs=(
            P("dp", None),
            P("dp", None),
            P("dp", "tensor"),
            P("dp", "tensor"),
            P("dp", "tensor"),
            P("tensor"),
            P("tensor"),
            P("tensor", "dp"),
            P(),
            P(),
            P(),
            P("dp", "tensor"),
            P("tensor"),
            P("tensor", "dp"),
            P(),
            P(),
            P(),
        ),
        check_vma=False,
    )
```

```python
import functools

import jax
import jax.numpy as jnp
from jax import lax
from jax.experimental import pallas as pl
from jax.experimental.pallas import tpu as pltpu
from jax.sharding import PartitionSpec as P

HEAD_DIM = 128
SLOT = 2048
LOG2E = 1.4426950408889634

norm_eps = 1e-12

F32 = jnp.float32
LOW = jnp.bfloat16
BOTH_LAST = (((1,), (1,)), ((), ()))
BOTH_FIRST = (((0,), (0,)), ((), ()))


def gelu_tanh(inner):
    return 0.5 * inner * (1.0 + jnp.tanh(0.7978845608 * (inner + 0.044715 * inner * inner * inner)))


def mat_bf(left, right):
    return jnp.dot(left, right, preferred_element_type=F32)


def mat_last(left, right):
    return lax.dot_general(left, right, BOTH_LAST, preferred_element_type=F32)


def mat_first(left, right):
    return lax.dot_general(left, right, BOTH_FIRST, preferred_element_type=F32)


def swap(value, axis, flip):
    count = lax.axis_size(axis)
    return lax.ppermute(value, axis, [(source, source ^ flip) for source in range(count)])


def after(value, *others):
    return lax.optimization_barrier((value, *others))[0]


def everyone(value, axes):
    for axis in axes:
        flip = 1
        while flip < lax.axis_size(axis):
            value = value + swap(value, axis, flip)
            flip *= 2
    return value


def gated(value, gate):
    return value if gate is None else after(value, gate)


def gather_near(block):
    return swap(block, "tensor", 1), swap(block, "tensor", 2)


def gather_rest(block, near):
    one, two = near
    half = block.shape[0] // 2
    rest = [swap(two[:half], "tensor", 1), swap(one[half:], "tensor", 2)]
    count, flip = lax.axis_size("tensor"), 4
    while flip < count:
        rest.append(swap(jnp.concatenate([block, one, two, *rest]), "tensor", flip))
        flip *= 2
    return rest


def gather_rows(block):
    near = gather_near(block)
    return jnp.concatenate([block, *near, *gather_rest(block, near)])


def scatter_rows(part, after_first=(), after_second=()):
    count = lax.axis_size("tensor")
    flip = count // 2
    extra = None
    while flip >= 4:
        away = jnp.concatenate([part(k, None) for k in range(flip, 2 * flip)])
        split = away.shape[0]
        if extra is not None:
            away = away + extra[split:].astype(F32)
        come = swap(away.astype(LOW), "tensor", flip)
        extra = come if extra is None else extra[:split].astype(F32) + come.astype(F32)
        flip //= 2

    def piece(k, gate=None):
        value = part(k, gate)
        if extra is not None:
            block = value.shape[0]
            value = value + extra[k * block : (k + 1) * block].astype(F32)
        return value

    three = piece(3).astype(LOW)
    half = three.shape[0] // 2
    come_top, come_low = swap(three[:half], "tensor", 1), swap(three[half:], "tensor", 2)
    one, two = piece(1, three), piece(2, three)
    first = [make(three) for make in after_first]
    come_top, come_low = after((come_top, come_low), *first)
    one = jnp.concatenate([one[:half].astype(LOW), (one[half:] + come_low.astype(F32)).astype(LOW)])
    two = jnp.concatenate([(two[:half] + come_top.astype(F32)).astype(LOW), two[half:].astype(LOW)])
    from_one, from_two = swap(one, "tensor", 1), swap(two, "tensor", 2)
    here = piece(0, (one, two))
    second = [make((one, two)) for make in after_second]
    from_one, from_two = after((from_one, from_two), here, *second)
    return (here, from_one, from_two), first, second


def normed(resid):
    center = resid - jnp.mean(resid, axis=-1, keepdims=True)
    spread = jnp.mean(center * center, axis=-1, keepdims=True)
    scale = lax.rsqrt(spread + norm_eps)
    return center * scale, scale


def norm_grad(unit, scale, grad, gain):
    inner = grad * gain
    back = scale * (
        inner
        - jnp.mean(inner, axis=-1, keepdims=True)
        - unit * jnp.mean(inner * unit, axis=-1, keepdims=True)
    )
    return back, grad * unit


def add_sums(sum_ref, *terms):
    @pl.when(pl.program_id(0) == 0)
    def _():
        sum_ref[...] = jnp.zeros_like(sum_ref)

    for row, term in enumerate(terms):
        sum_ref[row : row + 1, :] += jnp.sum(term, axis=0, keepdims=True)


def received(here_ref, one_ref, two_ref):
    return here_ref[...] + one_ref[...].astype(F32) + two_ref[...].astype(F32)


def norm_one_kernel(
    in_ref, h, one, two, b_ref, gain_ref, shift_ref, resid_ref, hidden_ref, low_ref
):
    resid = in_ref[...].astype(F32) + (received(h, one, two) + b_ref[...])
    unit, _ = normed(resid)
    hidden = unit * gain_ref[...] + shift_ref[...]
    resid_ref[...] = resid
    hidden_ref[...] = hidden
    low_ref[...] = hidden.astype(LOW)


def norm_two_kernel(
    hidden_ref, h, one, two, b_ref, gain_ref, shift_ref, cot_ref, live_ref,
    grad_ref, low_ref, out_ref, sum_ref,
):
    unit, scale = normed(hidden_ref[...] + (received(h, one, two) + b_ref[...]))
    gain = gain_ref[...]
    out_ref[...] = (unit * gain + shift_ref[...]).astype(LOW)
    grad = cot_ref[...].astype(F32) * live_ref[:, 0:1]
    back, to_gain = norm_grad(unit, scale, grad, gain)
    grad_ref[...] = back
    low_ref[...] = back.astype(LOW)
    add_sums(sum_ref, back, to_gain, grad)


def norm_one_back_kernel(
    resid_ref, grad_ref, h, one, two, gain_ref, back_ref, low_ref, sum_ref
):
    grad = grad_ref[...] + received(h, one, two)
    unit, scale = normed(resid_ref[...])
    back, to_gain = norm_grad(unit, scale, grad, gain_ref[...])
    back_ref[...] = back
    low_ref[...] = back.astype(LOW)
    add_sums(sum_ref, back, to_gain, grad)


def on_rows(kernel, name, args, outs, sums, tile=64):
    rows, model = args[0].shape
    tile = min(tile, rows)

    def spec(shape):
        if shape[0] == 1:
            return pl.BlockSpec(shape, lambda i: (0, 0))
        return pl.BlockSpec((tile, shape[1]), lambda i: (i, 0))

    out_shape = [jax.ShapeDtypeStruct((rows, model), dtype) for dtype in outs]
    out_specs = [spec(out.shape) for out in out_shape]
    if sums:
        out_shape.append(jax.ShapeDtypeStruct((8, model), F32))
        out_specs.append(pl.BlockSpec((8, model), lambda i: (0, 0)))
    return pl.pallas_call(
        kernel,
        grid=(rows // tile,),
        in_specs=[spec(arg.shape) for arg in args],
        out_specs=out_specs,
        out_shape=out_shape,
        compiler_params=pltpu.CompilerParams(vmem_limit_bytes=32 << 20),
        cost_estimate=pl.CostEstimate(
            flops=20 * rows * model, transcendentals=rows, bytes_accessed=20 * rows * model
        ),
        name=name,
    )(*args)


def fwd_kernel(q_ref,ko_ref,kf_ref,vo_ref,vf_ref,bo_ref,bf_ref,o_ref,l_ref,*,scale):
    q=q_ref[...]
    so=lax.dot_general(q,ko_ref[...],BOTH_LAST,preferred_element_type=F32)*scale+bo_ref[...]
    sf=lax.dot_general(q,kf_ref[...],BOTH_LAST,preferred_element_type=F32)*scale+bf_ref[...]
    top=jnp.maximum(jnp.max(so,axis=1,keepdims=True),jnp.max(sf,axis=1,keepdims=True))
    po=jnp.exp2(so-top); pf=jnp.exp2(sf-top)
    tot=jnp.sum(po,axis=1,keepdims=True)+jnp.sum(pf,axis=1,keepdims=True)
    o=jnp.dot(po.astype(LOW),vo_ref[...],preferred_element_type=F32)+jnp.dot(pf.astype(LOW),vf_ref[...],preferred_element_type=F32)
    o_ref[...]=(o/tot).astype(LOW)
    lse=top+jnp.log2(tot)
    l_ref[0]=jnp.transpose(jnp.broadcast_to(lse,(lse.shape[0],HEAD_DIM)))[0:1,:]
def attn_fwd(qkv,kv_far,bias_own,bias_far,heads,bq=256):
    rows=qkv.shape[0]
    scale=LOG2E*HEAD_DIM**-0.5
    return pl.pallas_call(
        functools.partial(fwd_kernel,scale=scale),
        grid=(heads,rows//bq),
        in_specs=[pl.BlockSpec((bq,HEAD_DIM),lambda h,i:(i,h)),
          pl.BlockSpec((rows,HEAD_DIM),lambda h,i:(0,heads+h)),
          pl.BlockSpec((rows,HEAD_DIM),lambda h,i:(0,h)),
          pl.BlockSpec((rows,HEAD_DIM),lambda h,i:(0,2*heads+h)),
          pl.BlockSpec((rows,HEAD_DIM),lambda h,i:(0,heads+h)),
          pl.BlockSpec((1,rows),lambda h,i:(0,0)),
          pl.BlockSpec((1,rows),lambda h,i:(0,0))],
        out_specs=[pl.BlockSpec((bq,HEAD_DIM),lambda h,i:(i,h)),pl.BlockSpec((1,1,bq),lambda h,i:(h,0,i))],
        out_shape=[jax.ShapeDtypeStruct((rows,heads*HEAD_DIM),LOW),jax.ShapeDtypeStruct((heads,1,rows),F32)],
        compiler_params=pltpu.CompilerParams(vmem_limit_bytes=48<<20),
        cost_estimate=pl.CostEstimate(flops=12*rows*2*rows*HEAD_DIM*heads,transcendentals=heads*rows*2*rows,bytes_accessed=heads*HEAD_DIM*rows*2*6),
        name='attention_forward')(qkv,qkv,kv_far,qkv,kv_far,bias_own,bias_far)

def bwd_kernel(q_ref,do_ref,o_ref,l_ref,ko_ref,kf_ref,vo_ref,vf_ref,bo_ref,bf_ref,dq_ref,dko_ref,dvo_ref,dkf_ref,
               ako,avo,akf,avf,kto,ktf,*,scale,chunk):
    i=pl.program_id(1); last=pl.num_programs(1)-1
    @pl.when(i==0)
    def _():
        kto[...]=jnp.transpose(ko_ref[...]); ktf[...]=jnp.transpose(kf_ref[...])
        for a in (ako,avo,akf,avf): a[...]=jnp.zeros_like(a)
    q=q_ref[...]; do=do_ref[...]
    lse=l_ref[0]
    delta=jnp.sum(jnp.transpose(do.astype(F32)*o_ref[...].astype(F32)),axis=0,keepdims=True)
    rows=ko_ref.shape[0]; bq=q.shape[0]
    dqt=jnp.zeros((HEAD_DIM,bq),F32)
    for k_ref,v_ref,b_ref,ak,av,kt in ((ko_ref,vo_ref,bo_ref,ako,avo,kto),(kf_ref,vf_ref,bf_ref,akf,avf,ktf)):
        for c in range(rows//chunk):
            sl=pl.ds(c*chunk,chunk)
            st=lax.dot_general(k_ref[sl,:],q,BOTH_LAST,preferred_element_type=F32)
            b=b_ref[sl,:]
            b=jnp.concatenate([b]*(bq//HEAD_DIM),axis=1)
            p=jnp.exp2(st*scale+b-lse)
            dp=lax.dot_general(v_ref[sl,:],do,BOTH_LAST,preferred_element_type=F32)
            ds=(p*(dp-delta)).astype(LOW)
            av[sl,:]+=jnp.dot(p.astype(LOW),do,preferred_element_type=F32)
            ak[sl,:]+=jnp.dot(ds,q,preferred_element_type=F32)
            dqt=dqt+jnp.dot(kt[:,sl],ds,preferred_element_type=F32)
    s=HEAD_DIM**-0.5
    dq_ref[...]=(jnp.transpose(dqt)*s).astype(LOW)
    @pl.when(i==last)
    def _():
        dko_ref[...]=ako[...]*s; dvo_ref[...]=avo[...]
        dkf_ref[0]=(akf[...]*s).astype(LOW); dkf_ref[1]=avf[...].astype(LOW)
def attn_bwd(qkv,kv_far,do,o,lse,bias_own,bias_far,heads,bq=256,chunk=512):
    rows=qkv.shape[0]
    scale=LOG2E*HEAD_DIM**-0.5
    full=lambda off: pl.BlockSpec((rows,HEAD_DIM),lambda h,i:(0,off+h))
    qb=pl.BlockSpec((bq,HEAD_DIM),lambda h,i:(i,h))
    return pl.pallas_call(
        functools.partial(bwd_kernel,scale=scale,chunk=chunk),
        grid=(heads,rows//bq),
        in_specs=[qb,qb,qb,pl.BlockSpec((1,1,bq),lambda h,i:(h,0,i)),
          full(heads),full(0),full(2*heads),full(heads),
          pl.BlockSpec((rows,HEAD_DIM),lambda h,i:(0,0)),pl.BlockSpec((rows,HEAD_DIM),lambda h,i:(0,0))],
        out_specs=[qb,full(0),full(0),pl.BlockSpec((2,rows,HEAD_DIM),lambda h,i:(0,0,h))],
        out_shape=[jax.ShapeDtypeStruct((rows,heads*HEAD_DIM),LOW)]+[jax.ShapeDtypeStruct((rows,heads*HEAD_DIM),F32)]*2+[jax.ShapeDtypeStruct((2,rows,heads*HEAD_DIM),LOW)],
        scratch_shapes=[pltpu.VMEM((rows,HEAD_DIM),F32)]*4+[pltpu.VMEM((HEAD_DIM,rows),LOW)]*2,
        compiler_params=pltpu.CompilerParams(vmem_limit_bytes=48<<20),
        cost_estimate=pl.CostEstimate(flops=20*rows*2*rows*HEAD_DIM*heads,transcendentals=heads*rows*2*rows,bytes_accessed=heads*HEAD_DIM*rows*2*12),
        name='attention_backward')(qkv,do,o,lse,qkv,kv_far,qkv,kv_far,bias_own,bias_far)


def on_device(
    tokens,
    cotangent,
    seq_lengths,
    slot_seq,
    w_query,
    w_key,
    w_value,
    b_query,
    b_value,
    w_out,
    b_out,
    ln1_gain,
    ln1_bias,
    w_inner,
    b_inner,
    w_outer,
    b_outer,
    ln2_gain,
    ln2_bias,
):
    tok_rows, model = tokens.shape
    assert SLOT == 2 * tok_rows
    tensor_count = lax.axis_size("tensor")
    tensor_place = lax.axis_index("tensor")
    block = tok_rows // tensor_count
    width_here = w_query.shape[1]
    heads_here = width_here // HEAD_DIM
    dp_place = lax.axis_index("dp")
    my_slot = dp_place // 2
    my_spot = dp_place % 2
    slot_ids = jnp.arange(slot_seq.shape[0])
    slot_lengths = jnp.sum(
        jnp.where(slot_seq[:, None] == slot_ids[None, :], seq_lengths[None, :], 0), axis=1
    )
    my_length = jnp.sum(jnp.where(slot_ids == my_slot, slot_lengths, 0))
    row_ids = jnp.arange(tok_rows)
    place = ((row_ids // block) ^ tensor_place) * block + row_ids % block
    own_bias = jnp.where(my_spot * tok_rows + place < my_length, 0.0, -1e30).astype(F32)
    far_bias = jnp.where((1 - my_spot) * tok_rows + place < my_length, 0.0, -1e30).astype(F32)
    own_bias_wide = jnp.broadcast_to(own_bias[:, None], (tok_rows, HEAD_DIM))
    far_bias_wide = jnp.broadcast_to(far_bias[:, None], (tok_rows, HEAD_DIM))

    def my_block(value):
        return lax.dynamic_slice_in_dim(value, tensor_place * block, block, 0)

    def reorder(value):
        return jnp.concatenate(
            [
                lax.dynamic_slice_in_dim(value, (tensor_place ^ k) * block, block, 0)
                for k in range(tensor_count)
            ]
        )

    row_live = (my_spot * tok_rows + place[:block] < my_length).astype(F32)
    rows_in = reorder(tokens)
    in_here = my_block(tokens)
    grad_out = my_block(cotangent)
    live_wide = jnp.broadcast_to(row_live[:, None], (block, HEAD_DIM))

    dp_count = lax.axis_size("dp")
    column = model // dp_count

    def columns_of(value, core):
        return jnp.concatenate(
            [
                jnp.where(
                    core == 0,
                    value[:, first : first + column],
                    value[:, first + column : first + 2 * column],
                )
                for first in range(0, model, 2 * column)
            ],
            axis=1,
        )

    def shared_columns(value):
        return columns_of(value, my_spot), swap(columns_of(value, 1 - my_spot), "dp", 1)

    def weight_grad(pairs):
        total = None
        for left, right in pairs:
            term = mat_first(left, right)
            total = term if total is None else total + term
        return total

    core_groups = [[core + 2 * step for step in range(dp_count // 2)] for core in range(2)]

    def to_owner(grad):
        return lax.psum_scatter(
            grad, "dp", scatter_dimension=0, tiled=True, axis_index_groups=core_groups
        )

    def split_rows(value):
        return [value[k * block : (k + 1) * block] for k in range(value.shape[0] // block)]

    low_attn = jnp.concatenate([w_query, w_key, w_value, w_out.T], axis=1).astype(LOW)
    low_inner = w_inner.T.astype(LOW)
    low_outer = w_outer.astype(LOW)
    full_attn = lax.all_gather(low_attn, "dp", axis=0, tiled=True)
    full_qkv, full_out = full_attn[:, : 3 * width_here], full_attn[:, 3 * width_here :].T
    full_inner = lax.all_gather(low_inner, "dp", axis=1, tiled=True)
    full_outer = lax.all_gather(low_outer, "dp", axis=1, tiled=True)

    rows_pair = shared_columns(rows_in)
    b_qkv = jnp.concatenate([b_query, jnp.zeros_like(b_query), b_value])
    qkv = (mat_bf(after(rows_in, rows_pair), full_qkv) + b_qkv).astype(LOW)
    far_kv = swap(qkv[:, width_here:], "dp", 1)
    mixed, lse = attn_fwd(qkv, far_kv, own_bias[None], far_bias[None], heads_here)

    mixed_blocks = split_rows(mixed)
    attn_parts, _, _ = scatter_rows(lambda k, gate: mat_bf(gated(mixed_blocks[k], gate), full_out))
    resid_one, hidden, hidden_here = on_rows(
        norm_one_kernel,
        "norm_one",
        (in_here, *attn_parts, b_out[None], ln1_gain[None], ln1_bias[None]),
        (F32, F32, LOW),
        False,
    )
    hidden_low = gather_rows(hidden_here)
    inner = mat_last(hidden_low, full_inner) + b_inner
    act, act_slope = jax.jvp(gelu_tanh, (inner,), (jnp.ones_like(inner),))
    act_low, act_slope = act.astype(LOW), act_slope.astype(LOW)
    mixed_far = swap(after(mixed, hidden_low), "dp", 1)
    hidden_pair = shared_columns(after(hidden_low, act_low))
    act_far = swap(act_low, "dp", 1)
    act_low, act_slope = after((act_low, act_slope), mixed_far, act_far, hidden_pair)

    act_blocks = split_rows(act_low)
    outer_parts, _, _ = scatter_rows(lambda k, gate: mat_bf(gated(act_blocks[k], gate), full_outer))
    grad_two, outer_here, output, sums_two = on_rows(
        norm_two_kernel,
        "norm_two",
        (
            hidden,
            *outer_parts,
            b_outer[None],
            ln2_gain[None],
            ln2_bias[None],
            grad_out,
            live_wide,
        ),
        (F32, LOW, LOW),
        True,
    )
    near = 3 * block
    outer_near = gather_near(outer_here)

    def act_grad(rows, first):
        slope = act_slope[first * block : first * block + rows.shape[0]]
        return (mat_last(rows, full_outer) * slope.astype(F32)).astype(LOW)

    inner_here = act_grad(outer_here, 0)
    outer_near = after(outer_near, inner_here)
    outer_rest = gather_rest(outer_here, outer_near)
    near_mine, near_far = shared_columns(jnp.concatenate([outer_here, *outer_near]))
    grad_near = weight_grad([(near_mine, act_low[:near]), (near_far, act_far[:near])])
    outer_rest = after(outer_rest, grad_near)
    outer_rest = jnp.concatenate(outer_rest)
    rest_mine, rest_far = shared_columns(outer_rest)
    grad_w_outer = (
        grad_near + weight_grad([(rest_mine, act_low[near:]), (rest_far, act_far[near:])])
    ).astype(LOW)
    owner_outer = to_owner(grad_w_outer)
    away_rows = jnp.concatenate([*outer_near, after(outer_rest, grad_w_outer)])
    inner_away = act_grad(away_rows, 1)
    inner_low = jnp.concatenate([inner_here, inner_away])
    inner_far = swap(inner_low, "dp", 1)
    inner_blocks = [inner_here, *split_rows(inner_away)]


    def inner_part(k, gate):
        return mat_bf(gated(inner_blocks[k], gate), full_inner)

    def inner_weight(sent):
        mine, far = after((inner_low, inner_far), sent)
        return weight_grad([(hidden_pair[0], mine), (hidden_pair[1], far)]).astype(LOW)

    hidden_parts, _, (grad_w_inner,) = scatter_rows(inner_part, (), [inner_weight])
    grad_one, attn_here, sums_one = on_rows(
        norm_one_back_kernel,
        "norm_one_back",
        (resid_one, grad_two, *hidden_parts, ln1_gain[None]),
        (F32, LOW),
        True,
    )
    owner_inner = to_owner(after(grad_w_inner, owner_outer, attn_here))
    attn_low = gather_rows(attn_here)
    mixed_low = mat_last(attn_low, full_out).astype(LOW)
    output = after(output, attn_low)
    query_low, own_key, own_value, far_pair = attn_bwd(
        qkv, far_kv, mixed_low, mixed, lse, own_bias_wide, far_bias_wide, heads_here, 512, 256
    )
    output_near = after(gather_near(output), query_low)
    output_rest = gather_rest(output, output_near)
    attn_pair = shared_columns(after(attn_low, query_low))
    far_key, far_value = after(swap(far_pair, "dp", 1), attn_pair).astype(F32)
    key_low = (own_key + far_key).astype(LOW)
    value_low = (own_value + far_value).astype(LOW)
    qkv_low = jnp.concatenate([query_low, key_low, value_low], axis=1)
    qkv_far = swap(qkv_low, "dp", 1)
    qkv_blocks = split_rows(qkv_low)

    def attn_weight(sent):
        mine, far = after((qkv_low, qkv_far), sent, owner_inner)
        grad_w_qkv = weight_grad([(rows_pair[0], mine), (rows_pair[1], far)]).astype(LOW)
        attn_mine, attn_far = after(attn_pair, grad_w_qkv)
        grad_w_out = weight_grad([(attn_mine, mixed), (attn_far, mixed_far)]).astype(LOW)
        return jnp.concatenate([grad_w_qkv, grad_w_out], axis=1)

    (here, one, two), (grad_w_attn, output_rest), _ = scatter_rows(
        lambda k, gate: mat_last(gated(qkv_blocks[k], gate), full_qkv), after_first=[attn_weight, lambda sent: output_rest]
    )
    owner_attn = to_owner(after(grad_w_attn, owner_inner))
    tokens_here = (grad_one + (here + one.astype(F32) + two.astype(F32))).astype(LOW)
    grad_tokens = gather_rows(tokens_here)
    output = jnp.concatenate([output, *output_near, *output_rest])
    output, grad_tokens = (reorder(rows).astype(F32) for rows in (output, grad_tokens))

    over_rows = jnp.concatenate([sums_one[:3], sums_two[:3]])
    over_rows = everyone(after(over_rows, tokens_here), ("tensor",)).reshape(-1)
    inner_sum = jnp.sum(inner_low.astype(F32), axis=0)
    qkv_sum = jnp.sum(qkv_low.astype(F32), axis=0)
    sums = everyone(jnp.concatenate([over_rows, inner_sum, qkv_sum]), ("dp",))
    grad_b_out, grad_ln1_gain, grad_ln1_bias, grad_b_outer, grad_ln2_gain, grad_ln2_bias = sums[
        : 6 * model
    ].reshape(6, model)
    grad_b_inner = sums[6 * model : -3 * width_here]
    grad_b_qkv = sums[-3 * width_here :]

    grad_w_outer, grad_w_inner, grad_w_attn = (
        grad.astype(F32) for grad in (owner_outer, owner_inner, owner_attn)
    )
    grad_w_query, grad_w_key, grad_w_value, grad_w_out = jnp.split(grad_w_attn, 4, axis=1)
    return (
        output,
        grad_tokens,
        grad_w_query,
        grad_w_key,
        grad_w_value,
        grad_b_qkv[:width_here],
        grad_b_qkv[2 * width_here :],
        grad_w_out.T,
        grad_b_out,
        grad_ln1_gain,
        grad_ln1_bias,
        grad_w_inner,
        grad_b_inner,
        grad_w_outer.T,
        grad_b_outer,
        grad_ln2_gain,
        grad_ln2_bias,
    )


def solution(mesh):
    return jax.shard_map(
        on_device,
        mesh=mesh,
        in_specs=(
            P("dp", None),
            P("dp", None),
            P(),
            P(),
            P("dp", "tensor"),
            P("dp", "tensor"),
            P("dp", "tensor"),
            P("tensor"),
            P("tensor"),
            P("tensor", "dp"),
            P(),
            P(),
            P(),
            P("dp", "tensor"),
            P("tensor"),
            P("tensor", "dp"),
            P(),
            P(),
            P(),
        ),
        out_specs=(
            P("dp", None),
            P("dp", None),
            P("dp", "tensor"),
            P("dp", "tensor"),
            P("dp", "tensor"),
            P("tensor"),
            P("tensor"),
            P("tensor", "dp"),
            P(),
            P(),
            P(),
            P("dp", "tensor"),
            P("tensor"),
            P("tensor", "dp"),
            P(),
            P(),
            P(),
        ),
        check_vma=False,
    )
```

```python
import functools

import jax
import jax.numpy as jnp
from jax import lax
from jax.experimental import pallas as pl
from jax.experimental.pallas import tpu as pltpu
from jax.sharding import PartitionSpec as P

HEAD_DIM = 128
SLOT = 2048
LOG2E = 1.4426950408889634

norm_eps = 1e-12

F32 = jnp.float32
LOW = jnp.bfloat16
BOTH_LAST = (((1,), (1,)), ((), ()))
BOTH_FIRST = (((0,), (0,)), ((), ()))


def gelu_tanh(inner):
    return 0.5 * inner * (1.0 + jnp.tanh(0.7978845608 * (inner + 0.044715 * inner * inner * inner)))


def mat_bf(left, right):
    return jnp.dot(left, right, preferred_element_type=F32)


def mat_last(left, right):
    return lax.dot_general(left, right, BOTH_LAST, preferred_element_type=F32)


def mat_first(left, right):
    return lax.dot_general(left, right, BOTH_FIRST, preferred_element_type=F32)


def swap(value, axis, flip):
    count = lax.axis_size(axis)
    return lax.ppermute(value, axis, [(source, source ^ flip) for source in range(count)])


def after(value, *others):
    return lax.optimization_barrier((value, *others))[0]


def everyone(value, axes):
    for axis in axes:
        flip = 1
        while flip < lax.axis_size(axis):
            value = value + swap(value, axis, flip)
            flip *= 2
    return value


def gated(value, gate):
    return value if gate is None else after(value, gate)


def gather_near(block):
    return swap(block, "tensor", 1), swap(block, "tensor", 2)


def gather_rest(block, near):
    one, two = near
    half = block.shape[0] // 2
    rest = [swap(two[:half], "tensor", 1), swap(one[half:], "tensor", 2)]
    count, flip = lax.axis_size("tensor"), 4
    while flip < count:
        rest.append(swap(jnp.concatenate([block, one, two, *rest]), "tensor", flip))
        flip *= 2
    return rest


def gather_rows(block):
    near = gather_near(block)
    return jnp.concatenate([block, *near, *gather_rest(block, near)])


def scatter_rows(part, after_first=(), after_second=()):
    count = lax.axis_size("tensor")
    flip = count // 2
    extra = None
    while flip >= 4:
        away = jnp.concatenate([part(k, None) for k in range(flip, 2 * flip)])
        split = away.shape[0]
        if extra is not None:
            away = away + extra[split:].astype(F32)
        come = swap(away.astype(LOW), "tensor", flip)
        extra = come if extra is None else extra[:split].astype(F32) + come.astype(F32)
        flip //= 2

    def piece(k, gate=None):
        value = part(k, gate)
        if extra is not None:
            block = value.shape[0]
            value = value + extra[k * block : (k + 1) * block].astype(F32)
        return value

    three = piece(3).astype(LOW)
    half = three.shape[0] // 2
    come_top, come_low = swap(three[:half], "tensor", 1), swap(three[half:], "tensor", 2)
    first = [make(three) for make in after_first]
    one, two = piece(1, (three, *first)), piece(2, (three, *first))
    come_top, come_low = after((come_top, come_low), *first)
    one = jnp.concatenate([one[:half].astype(LOW), (one[half:] + come_low.astype(F32)).astype(LOW)])
    two = jnp.concatenate([(two[:half] + come_top.astype(F32)).astype(LOW), two[half:].astype(LOW)])
    from_one, from_two = swap(one, "tensor", 1), swap(two, "tensor", 2)
    here = piece(0, (one, two))
    second = [make((one, two)) for make in after_second]
    from_one, from_two = after((from_one, from_two), here, *jax.tree.leaves(second))
    return (here, from_one, from_two), first, second


def normed(resid):
    center = resid - jnp.mean(resid, axis=-1, keepdims=True)
    spread = jnp.mean(center * center, axis=-1, keepdims=True)
    scale = lax.rsqrt(spread + norm_eps)
    return center * scale, scale


def norm_grad(unit, scale, grad, gain):
    inner = grad * gain
    back = scale * (
        inner
        - jnp.mean(inner, axis=-1, keepdims=True)
        - unit * jnp.mean(inner * unit, axis=-1, keepdims=True)
    )
    return back, grad * unit


def add_sums(sum_ref, *terms):
    @pl.when(pl.program_id(0) == 0)
    def _():
        sum_ref[...] = jnp.zeros_like(sum_ref)

    for row, term in enumerate(terms):
        sum_ref[row : row + 1, :] += jnp.sum(term, axis=0, keepdims=True)


def received(here_ref, one_ref, two_ref):
    return here_ref[...] + one_ref[...].astype(F32) + two_ref[...].astype(F32)


def norm_one_kernel(
    in_ref, h, one, two, b_ref, gain_ref, shift_ref, resid_ref, hidden_ref, low_ref
):
    resid = in_ref[...].astype(F32) + (received(h, one, two) + b_ref[...])
    unit, _ = normed(resid)
    hidden = unit * gain_ref[...] + shift_ref[...]
    resid_ref[...] = resid
    hidden_ref[...] = hidden
    low_ref[...] = hidden.astype(LOW)


def norm_two_kernel(
    hidden_ref, h, one, two, b_ref, gain_ref, shift_ref, cot_ref, live_ref,
    grad_ref, low_ref, out_ref, sum_ref,
):
    unit, scale = normed(hidden_ref[...] + (received(h, one, two) + b_ref[...]))
    gain = gain_ref[...]
    out_ref[...] = (unit * gain + shift_ref[...]).astype(LOW)
    grad = cot_ref[...].astype(F32) * live_ref[:, 0:1]
    back, to_gain = norm_grad(unit, scale, grad, gain)
    grad_ref[...] = back
    low_ref[...] = back.astype(LOW)
    add_sums(sum_ref, back, to_gain, grad)


def norm_one_back_kernel(
    resid_ref, grad_ref, h, one, two, gain_ref, back_ref, low_ref, sum_ref
):
    grad = grad_ref[...] + received(h, one, two)
    unit, scale = normed(resid_ref[...])
    back, to_gain = norm_grad(unit, scale, grad, gain_ref[...])
    back_ref[...] = back
    low_ref[...] = back.astype(LOW)
    add_sums(sum_ref, back, to_gain, grad)


def on_rows(kernel, name, args, outs, sums, tile=64):
    rows, model = args[0].shape
    tile = min(tile, rows)

    def spec(shape):
        if shape[0] == 1:
            return pl.BlockSpec(shape, lambda i: (0, 0))
        return pl.BlockSpec((tile, shape[1]), lambda i: (i, 0))

    out_shape = [jax.ShapeDtypeStruct((rows, model), dtype) for dtype in outs]
    out_specs = [spec(out.shape) for out in out_shape]
    if sums:
        out_shape.append(jax.ShapeDtypeStruct((8, model), F32))
        out_specs.append(pl.BlockSpec((8, model), lambda i: (0, 0)))
    return pl.pallas_call(
        kernel,
        grid=(rows // tile,),
        in_specs=[spec(arg.shape) for arg in args],
        out_specs=out_specs,
        out_shape=out_shape,
        compiler_params=pltpu.CompilerParams(vmem_limit_bytes=32 << 20),
        cost_estimate=pl.CostEstimate(
            flops=20 * rows * model, transcendentals=rows, bytes_accessed=20 * rows * model
        ),
        name=name,
    )(*args)


def fwd_kernel(q_ref,ko_ref,kf_ref,vo_ref,vf_ref,bo_ref,bf_ref,o_ref,l_ref,*,scale):
    q=q_ref[...]
    so=lax.dot_general(q,ko_ref[...],BOTH_LAST,preferred_element_type=F32)*scale+bo_ref[...]
    sf=lax.dot_general(q,kf_ref[...],BOTH_LAST,preferred_element_type=F32)*scale+bf_ref[...]
    top=jnp.maximum(jnp.max(so,axis=1,keepdims=True),jnp.max(sf,axis=1,keepdims=True))
    po=jnp.exp2(so-top); pf=jnp.exp2(sf-top)
    tot=jnp.sum(po,axis=1,keepdims=True)+jnp.sum(pf,axis=1,keepdims=True)
    o=jnp.dot(po.astype(LOW),vo_ref[...],preferred_element_type=F32)+jnp.dot(pf.astype(LOW),vf_ref[...],preferred_element_type=F32)
    o_ref[...]=(o/tot).astype(LOW)
    lse=top+jnp.log2(tot)
    l_ref[0]=jnp.transpose(jnp.broadcast_to(lse,(lse.shape[0],HEAD_DIM)))[0:1,:]
def attn_fwd(qkv,kv_far,bias_own,bias_far,heads,bq=256):
    rows=qkv.shape[0]
    scale=LOG2E*HEAD_DIM**-0.5
    return pl.pallas_call(
        functools.partial(fwd_kernel,scale=scale),
        grid=(heads,rows//bq),
        in_specs=[pl.BlockSpec((bq,HEAD_DIM),lambda h,i:(i,h)),
          pl.BlockSpec((rows,HEAD_DIM),lambda h,i:(0,heads+h)),
          pl.BlockSpec((rows,HEAD_DIM),lambda h,i:(0,h)),
          pl.BlockSpec((rows,HEAD_DIM),lambda h,i:(0,2*heads+h)),
          pl.BlockSpec((rows,HEAD_DIM),lambda h,i:(0,heads+h)),
          pl.BlockSpec((1,rows),lambda h,i:(0,0)),
          pl.BlockSpec((1,rows),lambda h,i:(0,0))],
        out_specs=[pl.BlockSpec((bq,HEAD_DIM),lambda h,i:(i,h)),pl.BlockSpec((1,1,bq),lambda h,i:(h,0,i))],
        out_shape=[jax.ShapeDtypeStruct((rows,heads*HEAD_DIM),LOW),jax.ShapeDtypeStruct((heads,1,rows),F32)],
        compiler_params=pltpu.CompilerParams(vmem_limit_bytes=48<<20),
        cost_estimate=pl.CostEstimate(flops=12*rows*2*rows*HEAD_DIM*heads,transcendentals=heads*rows*2*rows,bytes_accessed=heads*HEAD_DIM*rows*2*6),
        name='attention_forward')(qkv,qkv,kv_far,qkv,kv_far,bias_own,bias_far)

def bwd_kernel(q_ref,do_ref,o_ref,l_ref,ko_ref,kf_ref,vo_ref,vf_ref,bo_ref,bf_ref,dq_ref,dko_ref,dvo_ref,dkf_ref,
               ako,avo,akf,avf,kto,ktf,*,scale,chunk):
    i=pl.program_id(1); last=pl.num_programs(1)-1
    @pl.when(i==0)
    def _():
        kto[...]=jnp.transpose(ko_ref[...]); ktf[...]=jnp.transpose(kf_ref[...])
        for a in (ako,avo,akf,avf): a[...]=jnp.zeros_like(a)
    q=q_ref[...]; do=do_ref[...]
    lse=l_ref[0]
    delta=jnp.sum(jnp.transpose(do.astype(F32)*o_ref[...].astype(F32)),axis=0,keepdims=True)
    rows=ko_ref.shape[0]; bq=q.shape[0]
    dqt=jnp.zeros((HEAD_DIM,bq),F32)
    for k_ref,v_ref,b_ref,ak,av,kt in ((ko_ref,vo_ref,bo_ref,ako,avo,kto),(kf_ref,vf_ref,bf_ref,akf,avf,ktf)):
        for c in range(rows//chunk):
            sl=pl.ds(c*chunk,chunk)
            st=lax.dot_general(k_ref[sl,:],q,BOTH_LAST,preferred_element_type=F32)
            b=b_ref[sl,:]
            b=jnp.concatenate([b]*(bq//HEAD_DIM),axis=1)
            p=jnp.exp2(st*scale+b-lse)
            dp=lax.dot_general(v_ref[sl,:],do,BOTH_LAST,preferred_element_type=F32)
            ds=(p*(dp-delta)).astype(LOW)
            av[sl,:]+=jnp.dot(p.astype(LOW),do,preferred_element_type=F32)
            ak[sl,:]+=jnp.dot(ds,q,preferred_element_type=F32)
            dqt=dqt+jnp.dot(kt[:,sl],ds,preferred_element_type=F32)
    s=HEAD_DIM**-0.5
    dq_ref[...]=(jnp.transpose(dqt)*s).astype(LOW)
    @pl.when(i==last)
    def _():
        dko_ref[...]=ako[...]*s; dvo_ref[...]=avo[...]
        dkf_ref[0]=(akf[...]*s).astype(LOW); dkf_ref[1]=avf[...].astype(LOW)
def attn_bwd(qkv,kv_far,do,o,lse,bias_own,bias_far,heads,bq=256,chunk=512):
    rows=qkv.shape[0]
    scale=LOG2E*HEAD_DIM**-0.5
    full=lambda off: pl.BlockSpec((rows,HEAD_DIM),lambda h,i:(0,off+h))
    qb=pl.BlockSpec((bq,HEAD_DIM),lambda h,i:(i,h))
    return pl.pallas_call(
        functools.partial(bwd_kernel,scale=scale,chunk=chunk),
        grid=(heads,rows//bq),
        in_specs=[qb,qb,qb,pl.BlockSpec((1,1,bq),lambda h,i:(h,0,i)),
          full(heads),full(0),full(2*heads),full(heads),
          pl.BlockSpec((rows,HEAD_DIM),lambda h,i:(0,0)),pl.BlockSpec((rows,HEAD_DIM),lambda h,i:(0,0))],
        out_specs=[qb,full(0),full(0),pl.BlockSpec((2,rows,HEAD_DIM),lambda h,i:(0,0,h))],
        out_shape=[jax.ShapeDtypeStruct((rows,heads*HEAD_DIM),LOW)]+[jax.ShapeDtypeStruct((rows,heads*HEAD_DIM),F32)]*2+[jax.ShapeDtypeStruct((2,rows,heads*HEAD_DIM),LOW)],
        scratch_shapes=[pltpu.VMEM((rows,HEAD_DIM),F32)]*4+[pltpu.VMEM((HEAD_DIM,rows),LOW)]*2,
        compiler_params=pltpu.CompilerParams(vmem_limit_bytes=48<<20),
        cost_estimate=pl.CostEstimate(flops=rows*heads,transcendentals=0,bytes_accessed=heads*HEAD_DIM*rows*2),
        name='attention_backward')(qkv,do,o,lse,qkv,kv_far,qkv,kv_far,bias_own,bias_far)


def on_device(
    tokens,
    cotangent,
    seq_lengths,
    slot_seq,
    w_query,
    w_key,
    w_value,
    b_query,
    b_value,
    w_out,
    b_out,
    ln1_gain,
    ln1_bias,
    w_inner,
    b_inner,
    w_outer,
    b_outer,
    ln2_gain,
    ln2_bias,
):
    tok_rows, model = tokens.shape
    assert SLOT == 2 * tok_rows
    tensor_count = lax.axis_size("tensor")
    tensor_place = lax.axis_index("tensor")
    block = tok_rows // tensor_count
    width_here = w_query.shape[1]
    heads_here = width_here // HEAD_DIM
    dp_place = lax.axis_index("dp")
    my_slot = dp_place // 2
    my_spot = dp_place % 2
    slot_ids = jnp.arange(slot_seq.shape[0])
    slot_lengths = jnp.sum(
        jnp.where(slot_seq[:, None] == slot_ids[None, :], seq_lengths[None, :], 0), axis=1
    )
    my_length = jnp.sum(jnp.where(slot_ids == my_slot, slot_lengths, 0))
    row_ids = jnp.arange(tok_rows)
    place = ((row_ids // block) ^ tensor_place) * block + row_ids % block
    own_bias = jnp.where(my_spot * tok_rows + place < my_length, 0.0, -1e30).astype(F32)
    far_bias = jnp.where((1 - my_spot) * tok_rows + place < my_length, 0.0, -1e30).astype(F32)
    own_bias_wide = jnp.broadcast_to(own_bias[:, None], (tok_rows, HEAD_DIM))
    far_bias_wide = jnp.broadcast_to(far_bias[:, None], (tok_rows, HEAD_DIM))

    def my_block(value):
        return lax.dynamic_slice_in_dim(value, tensor_place * block, block, 0)

    def reorder(value):
        return jnp.concatenate(
            [
                lax.dynamic_slice_in_dim(value, (tensor_place ^ k) * block, block, 0)
                for k in range(tensor_count)
            ]
        )

    row_live = (my_spot * tok_rows + place[:block] < my_length).astype(F32)
    rows_in = reorder(tokens)
    in_here = my_block(tokens)
    grad_out = my_block(cotangent)
    live_wide = jnp.broadcast_to(row_live[:, None], (block, HEAD_DIM))

    dp_count = lax.axis_size("dp")
    column = model // dp_count

    def columns_of(value, core):
        return jnp.concatenate(
            [
                jnp.where(
                    core == 0,
                    value[:, first : first + column],
                    value[:, first + column : first + 2 * column],
                )
                for first in range(0, model, 2 * column)
            ],
            axis=1,
        )

    def shared_columns(value):
        return columns_of(value, my_spot), swap(columns_of(value, 1 - my_spot), "dp", 1)

    def weight_grad(pairs):
        total = None
        for left, right in pairs:
            term = mat_first(left, right)
            total = term if total is None else total + term
        return total

    core_groups = [[core + 2 * step for step in range(dp_count // 2)] for core in range(2)]

    def to_owner(grad):
        return lax.psum_scatter(
            grad, "dp", scatter_dimension=0, tiled=True, axis_index_groups=core_groups
        )

    def rows_of(value, k):
        return value[k * block : (k + 1) * block]

    low_attn = jnp.concatenate([w_query, w_key, w_value, w_out.T], axis=1).astype(LOW)
    low_inner = w_inner.T.astype(LOW)
    low_outer = w_outer.astype(LOW)
    full_attn = lax.all_gather(low_attn, "dp", axis=0, tiled=True)
    full_qkv, full_out = full_attn[:, : 3 * width_here], full_attn[:, 3 * width_here :].T
    full_inner = lax.all_gather(low_inner, "dp", axis=1, tiled=True)
    full_outer = lax.all_gather(low_outer, "dp", axis=1, tiled=True)

    rows_pair = shared_columns(rows_in)
    b_qkv = jnp.concatenate([b_query, jnp.zeros_like(b_query), b_value])
    qkv = (mat_bf(after(rows_in, rows_pair), full_qkv) + b_qkv).astype(LOW)
    far_kv = swap(qkv[:, width_here:], "dp", 1)
    mixed, lse = attn_fwd(qkv, far_kv, own_bias[None], far_bias[None], heads_here)

    attn_parts, _, _ = scatter_rows(lambda k, gate: mat_bf(rows_of(gated(mixed, gate), k), full_out))
    resid_one, hidden, hidden_here = on_rows(
        norm_one_kernel,
        "norm_one",
        (in_here, *attn_parts, b_out[None], ln1_gain[None], ln1_bias[None]),
        (F32, F32, LOW),
        False,
    )
    hidden_low = gather_rows(hidden_here)
    inner = mat_last(hidden_low, full_inner) + b_inner
    act, act_slope = jax.jvp(gelu_tanh, (inner,), (jnp.ones_like(inner),))
    act_low, act_slope = act.astype(LOW), act_slope.astype(LOW)
    mixed_far = swap(after(mixed, hidden_low), "dp", 1)
    hidden_pair = shared_columns(after(hidden_low, act_low))
    act_far = swap(act_low, "dp", 1)
    act_low, act_slope = after((act_low, act_slope), mixed_far, act_far, hidden_pair)

    outer_parts, _, _ = scatter_rows(lambda k, gate: mat_bf(rows_of(gated(act_low, gate), k), full_outer))
    grad_two, outer_here, output, sums_two = on_rows(
        norm_two_kernel,
        "norm_two",
        (
            hidden,
            *outer_parts,
            b_outer[None],
            ln2_gain[None],
            ln2_bias[None],
            grad_out,
            live_wide,
        ),
        (F32, LOW, LOW),
        True,
    )
    near = 3 * block
    outer_near = gather_near(outer_here)

    def act_grad(rows, first):
        slope = act_slope[first * block : first * block + rows.shape[0]]
        return (mat_last(rows, full_outer) * slope.astype(F32)).astype(LOW)

    inner_here = act_grad(outer_here, 0)
    outer_near = after(outer_near, inner_here)
    outer_rest = gather_rest(outer_here, outer_near)
    near_mine, near_far = shared_columns(jnp.concatenate([outer_here, *outer_near]))
    grad_near = weight_grad([(near_mine, act_low[:near]), (near_far, act_far[:near])])
    outer_rest = after(outer_rest, grad_near)
    output_near = gather_near(after(output, *outer_rest))
    outer_rest = jnp.concatenate(outer_rest)
    rest_mine, rest_far = shared_columns(outer_rest)
    grad_w_outer = (
        grad_near + weight_grad([(rest_mine, act_low[near:]), (rest_far, act_far[near:])])
    ).astype(LOW)
    owner_outer = to_owner(grad_w_outer)
    away_rows = jnp.concatenate([*outer_near, after(outer_rest, grad_w_outer)])
    inner_away = act_grad(away_rows, 1)
    inner_low = jnp.concatenate([inner_here, inner_away])
    inner_far = swap(inner_low, "dp", 1)

    inner_three, output_near = lax.optimization_barrier(
        (mat_bf(rows_of(inner_away, 2), full_inner), output_near)
    )

    def inner_part(k, gate):
        if k == 3:
            return inner_three
        rows = inner_here if k == 0 else inner_away
        return mat_bf(rows_of(gated(rows, gate), max(k - 1, 0)), full_inner)

    def inner_weight(sent):
        mine, far = after((inner_low, inner_far), sent)
        return weight_grad([(hidden_pair[0], mine), (hidden_pair[1], far)]).astype(LOW)

    hidden_parts, _, (grad_w_inner,) = scatter_rows(inner_part, (), [inner_weight])
    grad_one, attn_here, sums_one = on_rows(
        norm_one_back_kernel,
        "norm_one_back",
        (resid_one, grad_two, *hidden_parts, ln1_gain[None]),
        (F32, LOW),
        True,
    )
    owner_inner = to_owner(after(grad_w_inner, owner_outer, attn_here))
    output_rest = gather_rest(output, after(output_near, *hidden_parts))
    attn_low = gather_rows(after(attn_here, output_rest))
    mixed_low = mat_last(attn_low, full_out).astype(LOW)
    query_low, own_key, own_value, far_pair = attn_bwd(
        qkv, far_kv, mixed_low, mixed, lse, own_bias_wide, far_bias_wide, heads_here, 512, 256
    )
    attn_pair = shared_columns(after(attn_low, query_low))
    far_key, far_value = after(swap(far_pair, "dp", 1), attn_pair).astype(F32)
    key_low = (own_key + far_key).astype(LOW)
    value_low = (own_value + far_value).astype(LOW)
    qkv_low = jnp.concatenate([query_low, key_low, value_low], axis=1)
    qkv_far = swap(qkv_low, "dp", 1)

    def attn_weight(sent):
        mine, far = after((qkv_low, qkv_far), sent, owner_inner)
        grad_w_qkv = weight_grad([(rows_pair[0], mine), (rows_pair[1], far)]).astype(LOW)
        attn_mine, attn_far = after(attn_pair, grad_w_qkv)
        grad_w_out = weight_grad([(attn_mine, mixed), (attn_far, mixed_far)]).astype(LOW)
        return jnp.concatenate([grad_w_qkv, grad_w_out], axis=1)

    def total_sums(sent):
        rows = jnp.concatenate([sums_one[:3], sums_two[:3]]).reshape(-1)
        inner_sum = jnp.sum(inner_low.astype(F32), axis=0)
        qkv_sum = jnp.sum(qkv_low.astype(F32), axis=0)
        return everyone(after(jnp.concatenate([rows, inner_sum, qkv_sum]), sent), ("dp",))

    def owned(sent):
        outer, inner = after((owner_outer, owner_inner), sent)
        return outer.T.astype(F32), inner.astype(F32)

    (here, one, two), (grad_w_attn,), (sums, (grad_w_outer, grad_w_inner)) = scatter_rows(
        lambda k, gate: mat_last(rows_of(gated(qkv_low, gate), k), full_qkv),
        after_first=[attn_weight],
        after_second=[total_sums, owned],
    )
    owner_attn = to_owner(after(grad_w_attn, owner_inner))
    tokens_here = (grad_one + (here + one.astype(F32) + two.astype(F32))).astype(LOW)
    tokens_near = gather_near(tokens_here)
    output = jnp.concatenate(after((output, *output_near, *output_rest), tokens_near))
    tokens_rest = gather_rest(tokens_here, tokens_near)
    grad_tokens = jnp.concatenate([tokens_here, *tokens_near, *tokens_rest])
    output, grad_tokens = (reorder(rows).astype(F32) for rows in (output, grad_tokens))

    grad_b_inner = sums[6 * model : -3 * width_here]
    grad_b_qkv = sums[-3 * width_here :]
    sums = everyone(after(sums[: 6 * model], tokens_rest), ("tensor",)).reshape(6, model)
    grad_b_out, grad_ln1_gain, grad_ln1_bias, grad_b_outer, grad_ln2_gain, grad_ln2_bias = sums

    grad_w_attn = owner_attn.astype(F32)
    grad_w_query, grad_w_key, grad_w_value, grad_w_out = jnp.split(grad_w_attn, 4, axis=1)
    return (
        output,
        grad_tokens,
        grad_w_query,
        grad_w_key,
        grad_w_value,
        grad_b_qkv[:width_here],
        grad_b_qkv[2 * width_here :],
        grad_w_out.T,
        grad_b_out,
        grad_ln1_gain,
        grad_ln1_bias,
        grad_w_inner,
        grad_b_inner,
        grad_w_outer,
        grad_b_outer,
        grad_ln2_gain,
        grad_ln2_bias,
    )


def solution(mesh):
    return jax.shard_map(
        on_device,
        mesh=mesh,
        in_specs=(
            P("dp", None),
            P("dp", None),
            P(),
            P(),
            P("dp", "tensor"),
            P("dp", "tensor"),
            P("dp", "tensor"),
            P("tensor"),
            P("tensor"),
            P("tensor", "dp"),
            P(),
            P(),
            P(),
            P("dp", "tensor"),
            P("tensor"),
            P("tensor", "dp"),
            P(),
            P(),
            P(),
        ),
        out_specs=(
            P("dp", None),
            P("dp", None),
            P("dp", "tensor"),
            P("dp", "tensor"),
            P("dp", "tensor"),
            P("tensor"),
            P("tensor"),
            P("tensor", "dp"),
            P(),
            P(),
            P(),
            P("dp", "tensor"),
            P("tensor"),
            P("tensor", "dp"),
            P(),
            P(),
            P(),
        ),
        check_vma=False,
    )
```

```python
import functools

import jax
import jax.numpy as jnp
from jax import lax
from jax.experimental import pallas as pl
from jax.experimental.pallas import tpu as pltpu
from jax.sharding import PartitionSpec as P

HEAD_DIM = 128
SLOT = 2048
LOG2E = 1.4426950408889634

norm_eps = 1e-12

F32 = jnp.float32
LOW = jnp.bfloat16
BOTH_LAST = (((1,), (1,)), ((), ()))
BOTH_FIRST = (((0,), (0,)), ((), ()))


def gelu_tanh(inner):
    return 0.5 * inner * (1.0 + jnp.tanh(0.7978845608 * (inner + 0.044715 * inner * inner * inner)))


def mat_bf(left, right):
    return jnp.dot(left, right, preferred_element_type=F32)


def mat_last(left, right):
    return lax.dot_general(left, right, BOTH_LAST, preferred_element_type=F32)


def mat_first(left, right):
    return lax.dot_general(left, right, BOTH_FIRST, preferred_element_type=F32)


def swap(value, axis, flip):
    count = lax.axis_size(axis)
    return lax.ppermute(value, axis, [(source, source ^ flip) for source in range(count)])


def after(value, *others):
    return lax.optimization_barrier((value, *others))[0]


def everyone(value, axes):
    for axis in axes:
        flip = 1
        while flip < lax.axis_size(axis):
            value = value + swap(value, axis, flip)
            flip *= 2
    return value


def gated(value, gate):
    return value if gate is None else after(value, gate)


def gather_near(block):
    return swap(block, "tensor", 1), swap(block, "tensor", 2)


def gather_rest(block, near):
    one, two = near
    half = block.shape[0] // 2
    rest = [swap(two[:half], "tensor", 1), swap(one[half:], "tensor", 2)]
    count, flip = lax.axis_size("tensor"), 4
    while flip < count:
        rest.append(swap(jnp.concatenate([block, one, two, *rest]), "tensor", flip))
        flip *= 2
    return rest


def gather_rows(block):
    near = gather_near(block)
    return jnp.concatenate([block, *near, *gather_rest(block, near)])


def scatter_rows(part, after_first=(), after_second=()):
    count = lax.axis_size("tensor")
    flip = count // 2
    extra = None
    while flip >= 4:
        away = part(flip, 2 * flip, None)
        split = away.shape[0]
        if extra is not None:
            away = away + extra[split:].astype(F32)
        come = swap(away.astype(LOW), "tensor", flip)
        extra = come if extra is None else extra[:split].astype(F32) + come.astype(F32)
        flip //= 2

    def piece(first, last, gate=None):
        value = part(first, last, gate)
        if extra is not None:
            block = extra.shape[0] // 4
            value = value + extra[first * block : last * block].astype(F32)
        return value

    three = piece(3, 4).astype(LOW)
    half = three.shape[0] // 2
    come_top, come_low = swap(three[:half], "tensor", 1), swap(three[half:], "tensor", 2)
    first = [make(three) for make in after_first]
    one, two = jnp.split(piece(1, 3, (three, *first)), 2)
    come_top, come_low = after((come_top, come_low), *first)
    one = jnp.concatenate([one[:half].astype(LOW), (one[half:] + come_low.astype(F32)).astype(LOW)])
    two = jnp.concatenate([(two[:half] + come_top.astype(F32)).astype(LOW), two[half:].astype(LOW)])
    from_one, from_two = swap(one, "tensor", 1), swap(two, "tensor", 2)
    here = piece(0, 1, (one, two))
    second = [make((one, two)) for make in after_second]
    from_one, from_two = after((from_one, from_two), here, *jax.tree.leaves(second))
    return (here, from_one, from_two), first, second


def normed(resid):
    center = resid - jnp.mean(resid, axis=-1, keepdims=True)
    spread = jnp.mean(center * center, axis=-1, keepdims=True)
    scale = lax.rsqrt(spread + norm_eps)
    return center * scale, scale


def norm_grad(unit, scale, grad, gain):
    inner = grad * gain
    back = scale * (
        inner
        - jnp.mean(inner, axis=-1, keepdims=True)
        - unit * jnp.mean(inner * unit, axis=-1, keepdims=True)
    )
    return back, grad * unit


def add_sums(sum_ref, *terms):
    @pl.when(pl.program_id(0) == 0)
    def _():
        sum_ref[...] = jnp.zeros_like(sum_ref)

    for row, term in enumerate(terms):
        sum_ref[row : row + 1, :] += jnp.sum(term, axis=0, keepdims=True)


def received(here_ref, one_ref, two_ref):
    return here_ref[...] + one_ref[...].astype(F32) + two_ref[...].astype(F32)


def norm_one_kernel(
    in_ref, h, one, two, b_ref, gain_ref, shift_ref, resid_ref, hidden_ref, low_ref
):
    resid = in_ref[...].astype(F32) + (received(h, one, two) + b_ref[...])
    unit, _ = normed(resid)
    hidden = unit * gain_ref[...] + shift_ref[...]
    resid_ref[...] = resid
    hidden_ref[...] = hidden
    low_ref[...] = hidden.astype(LOW)


def norm_two_kernel(
    hidden_ref, h, one, two, b_ref, gain_ref, shift_ref, cot_ref, live_ref,
    grad_ref, low_ref, out_ref, sum_ref,
):
    unit, scale = normed(hidden_ref[...] + (received(h, one, two) + b_ref[...]))
    gain = gain_ref[...]
    out_ref[...] = (unit * gain + shift_ref[...]).astype(LOW)
    grad = cot_ref[...].astype(F32) * live_ref[:, 0:1]
    back, to_gain = norm_grad(unit, scale, grad, gain)
    grad_ref[...] = back
    low_ref[...] = back.astype(LOW)
    add_sums(sum_ref, back, to_gain, grad)


def norm_one_back_kernel(
    resid_ref, grad_ref, h, one, two, gain_ref, back_ref, low_ref, sum_ref
):
    grad = grad_ref[...] + received(h, one, two)
    unit, scale = normed(resid_ref[...])
    back, to_gain = norm_grad(unit, scale, grad, gain_ref[...])
    back_ref[...] = back
    low_ref[...] = back.astype(LOW)
    add_sums(sum_ref, back, to_gain, grad)


def on_rows(kernel, name, args, outs, sums, tile=64):
    rows, model = args[0].shape
    tile = min(tile, rows)

    def spec(shape):
        if shape[0] == 1:
            return pl.BlockSpec(shape, lambda i: (0, 0))
        return pl.BlockSpec((tile, shape[1]), lambda i: (i, 0))

    out_shape = [jax.ShapeDtypeStruct((rows, model), dtype) for dtype in outs]
    out_specs = [spec(out.shape) for out in out_shape]
    if sums:
        out_shape.append(jax.ShapeDtypeStruct((8, model), F32))
        out_specs.append(pl.BlockSpec((8, model), lambda i: (0, 0)))
    return pl.pallas_call(
        kernel,
        grid=(rows // tile,),
        in_specs=[spec(arg.shape) for arg in args],
        out_specs=out_specs,
        out_shape=out_shape,
        compiler_params=pltpu.CompilerParams(vmem_limit_bytes=32 << 20),
        cost_estimate=pl.CostEstimate(
            flops=20 * rows * model, transcendentals=rows, bytes_accessed=20 * rows * model
        ),
        name=name,
    )(*args)


def fwd_kernel(q_ref,ko_ref,kf_ref,vo_ref,vf_ref,bo_ref,bf_ref,o_ref,l_ref,*,scale):
    q=q_ref[...]
    so=lax.dot_general(q,ko_ref[...],BOTH_LAST,preferred_element_type=F32)*scale+bo_ref[...]
    sf=lax.dot_general(q,kf_ref[...],BOTH_LAST,preferred_element_type=F32)*scale+bf_ref[...]
    top=jnp.maximum(jnp.max(so,axis=1,keepdims=True),jnp.max(sf,axis=1,keepdims=True))
    po=jnp.exp2(so-top); pf=jnp.exp2(sf-top)
    tot=jnp.sum(po,axis=1,keepdims=True)+jnp.sum(pf,axis=1,keepdims=True)
    o=jnp.dot(po.astype(LOW),vo_ref[...],preferred_element_type=F32)+jnp.dot(pf.astype(LOW),vf_ref[...],preferred_element_type=F32)
    o_ref[...]=(o/tot).astype(LOW)
    lse=top+jnp.log2(tot)
    l_ref[0]=jnp.transpose(jnp.broadcast_to(lse,(lse.shape[0],HEAD_DIM)))[0:1,:]
def attn_fwd(qkv,kv_far,bias_own,bias_far,heads,bq=256):
    rows=qkv.shape[0]
    scale=LOG2E*HEAD_DIM**-0.5
    return pl.pallas_call(
        functools.partial(fwd_kernel,scale=scale),
        grid=(heads,rows//bq),
        in_specs=[pl.BlockSpec((bq,HEAD_DIM),lambda h,i:(i,h)),
          pl.BlockSpec((rows,HEAD_DIM),lambda h,i:(0,heads+h)),
          pl.BlockSpec((rows,HEAD_DIM),lambda h,i:(0,h)),
          pl.BlockSpec((rows,HEAD_DIM),lambda h,i:(0,2*heads+h)),
          pl.BlockSpec((rows,HEAD_DIM),lambda h,i:(0,heads+h)),
          pl.BlockSpec((1,rows),lambda h,i:(0,0)),
          pl.BlockSpec((1,rows),lambda h,i:(0,0))],
        out_specs=[pl.BlockSpec((bq,HEAD_DIM),lambda h,i:(i,h)),pl.BlockSpec((1,1,bq),lambda h,i:(h,0,i))],
        out_shape=[jax.ShapeDtypeStruct((rows,heads*HEAD_DIM),LOW),jax.ShapeDtypeStruct((heads,1,rows),F32)],
        compiler_params=pltpu.CompilerParams(vmem_limit_bytes=48<<20),
        cost_estimate=pl.CostEstimate(flops=12*rows*2*rows*HEAD_DIM*heads,transcendentals=heads*rows*2*rows,bytes_accessed=heads*HEAD_DIM*rows*2*6),
        name='attention_forward')(qkv,qkv,kv_far,qkv,kv_far,bias_own,bias_far)

def bwd_kernel(q_ref,do_ref,o_ref,l_ref,ko_ref,kf_ref,vo_ref,vf_ref,bo_ref,bf_ref,dq_ref,dko_ref,dvo_ref,dkf_ref,
               ako,avo,akf,avf,kto,ktf,*,scale,chunk):
    i=pl.program_id(1); last=pl.num_programs(1)-1
    @pl.when(i==0)
    def _():
        kto[...]=jnp.transpose(ko_ref[...]); ktf[...]=jnp.transpose(kf_ref[...])
        for a in (ako,avo,akf,avf): a[...]=jnp.zeros_like(a)
    q=q_ref[...]; do=do_ref[...]
    lse=l_ref[0]
    delta=jnp.sum(jnp.transpose(do.astype(F32)*o_ref[...].astype(F32)),axis=0,keepdims=True)
    rows=ko_ref.shape[0]; bq=q.shape[0]
    dqt=jnp.zeros((HEAD_DIM,bq),F32)
    for k_ref,v_ref,b_ref,ak,av,kt in ((ko_ref,vo_ref,bo_ref,ako,avo,kto),(kf_ref,vf_ref,bf_ref,akf,avf,ktf)):
        for c in range(rows//chunk):
            sl=pl.ds(c*chunk,chunk)
            st=lax.dot_general(k_ref[sl,:],q,BOTH_LAST,preferred_element_type=F32)
            b=b_ref[sl,:]
            b=jnp.concatenate([b]*(bq//HEAD_DIM),axis=1)
            p=jnp.exp2(st*scale+b-lse)
            dp=lax.dot_general(v_ref[sl,:],do,BOTH_LAST,preferred_element_type=F32)
            ds=(p*(dp-delta)).astype(LOW)
            av[sl,:]+=jnp.dot(p.astype(LOW),do,preferred_element_type=F32)
            ak[sl,:]+=jnp.dot(ds,q,preferred_element_type=F32)
            dqt=dqt+jnp.dot(kt[:,sl],ds,preferred_element_type=F32)
    s=HEAD_DIM**-0.5
    dq_ref[...]=(jnp.transpose(dqt)*s).astype(LOW)
    @pl.when(i==last)
    def _():
        dko_ref[...]=ako[...]*s; dvo_ref[...]=avo[...]
        dkf_ref[0]=(akf[...]*s).astype(LOW); dkf_ref[1]=avf[...].astype(LOW)
def attn_bwd(qkv,kv_far,do,o,lse,bias_own,bias_far,heads,bq=256,chunk=512):
    rows=qkv.shape[0]
    scale=LOG2E*HEAD_DIM**-0.5
    full=lambda off: pl.BlockSpec((rows,HEAD_DIM),lambda h,i:(0,off+h))
    qb=pl.BlockSpec((bq,HEAD_DIM),lambda h,i:(i,h))
    return pl.pallas_call(
        functools.partial(bwd_kernel,scale=scale,chunk=chunk),
        grid=(heads,rows//bq),
        in_specs=[qb,qb,qb,pl.BlockSpec((1,1,bq),lambda h,i:(h,0,i)),
          full(heads),full(0),full(2*heads),full(heads),
          pl.BlockSpec((rows,HEAD_DIM),lambda h,i:(0,0)),pl.BlockSpec((rows,HEAD_DIM),lambda h,i:(0,0))],
        out_specs=[qb,full(0),full(0),pl.BlockSpec((2,rows,HEAD_DIM),lambda h,i:(0,0,h))],
        out_shape=[jax.ShapeDtypeStruct((rows,heads*HEAD_DIM),LOW)]+[jax.ShapeDtypeStruct((rows,heads*HEAD_DIM),F32)]*2+[jax.ShapeDtypeStruct((2,rows,heads*HEAD_DIM),LOW)],
        scratch_shapes=[pltpu.VMEM((rows,HEAD_DIM),F32)]*4+[pltpu.VMEM((HEAD_DIM,rows),LOW)]*2,
        compiler_params=pltpu.CompilerParams(vmem_limit_bytes=48<<20),
        cost_estimate=pl.CostEstimate(flops=rows*heads,transcendentals=0,bytes_accessed=heads*HEAD_DIM*rows*2),
        name='attention_backward')(qkv,do,o,lse,qkv,kv_far,qkv,kv_far,bias_own,bias_far)


def on_device(
    tokens,
    cotangent,
    seq_lengths,
    slot_seq,
    w_query,
    w_key,
    w_value,
    b_query,
    b_value,
    w_out,
    b_out,
    ln1_gain,
    ln1_bias,
    w_inner,
    b_inner,
    w_outer,
    b_outer,
    ln2_gain,
    ln2_bias,
):
    tok_rows, model = tokens.shape
    assert SLOT == 2 * tok_rows
    tensor_count = lax.axis_size("tensor")
    tensor_place = lax.axis_index("tensor")
    block = tok_rows // tensor_count
    width_here = w_query.shape[1]
    heads_here = width_here // HEAD_DIM
    dp_place = lax.axis_index("dp")
    my_slot = dp_place // 2
    my_spot = dp_place % 2
    slot_ids = jnp.arange(slot_seq.shape[0])
    slot_lengths = jnp.sum(
        jnp.where(slot_seq[:, None] == slot_ids[None, :], seq_lengths[None, :], 0), axis=1
    )
    my_length = jnp.sum(jnp.where(slot_ids == my_slot, slot_lengths, 0))
    row_ids = jnp.arange(tok_rows)
    place = ((row_ids // block) ^ tensor_place) * block + row_ids % block
    own_bias = jnp.where(my_spot * tok_rows + place < my_length, 0.0, -1e30).astype(F32)
    far_bias = jnp.where((1 - my_spot) * tok_rows + place < my_length, 0.0, -1e30).astype(F32)
    own_bias_wide = jnp.broadcast_to(own_bias[:, None], (tok_rows, HEAD_DIM))
    far_bias_wide = jnp.broadcast_to(far_bias[:, None], (tok_rows, HEAD_DIM))

    def my_block(value):
        return lax.dynamic_slice_in_dim(value, tensor_place * block, block, 0)

    def reorder(value):
        return jnp.concatenate(
            [
                lax.dynamic_slice_in_dim(value, (tensor_place ^ k) * block, block, 0)
                for k in range(tensor_count)
            ]
        )

    row_live = (my_spot * tok_rows + place[:block] < my_length).astype(F32)
    rows_in = reorder(tokens)
    in_here = my_block(tokens)
    grad_out = my_block(cotangent)
    live_wide = jnp.broadcast_to(row_live[:, None], (block, HEAD_DIM))

    dp_count = lax.axis_size("dp")
    column = model // dp_count

    def columns_of(value, core):
        return jnp.concatenate(
            [
                jnp.where(
                    core == 0,
                    value[:, first : first + column],
                    value[:, first + column : first + 2 * column],
                )
                for first in range(0, model, 2 * column)
            ],
            axis=1,
        )

    def shared_columns(value):
        return columns_of(value, my_spot), swap(columns_of(value, 1 - my_spot), "dp", 1)

    def weight_grad(pairs):
        total = None
        for left, right in pairs:
            term = mat_first(left, right)
            total = term if total is None else total + term
        return total

    core_groups = [[core + 2 * step for step in range(dp_count // 2)] for core in range(2)]

    def to_owner(grad):
        return lax.psum_scatter(
            grad, "dp", scatter_dimension=0, tiled=True, axis_index_groups=core_groups
        )

    def rows_of(value, first, last):
        return value[first * block : last * block]

    low_attn = jnp.concatenate([w_query, w_key, w_value, w_out.T], axis=1).astype(LOW)
    low_inner = w_inner.T.astype(LOW)
    low_outer = w_outer.astype(LOW)
    full_attn = lax.all_gather(low_attn, "dp", axis=0, tiled=True)
    full_qkv, full_out = full_attn[:, : 3 * width_here], full_attn[:, 3 * width_here :].T
    full_inner = lax.all_gather(low_inner, "dp", axis=1, tiled=True)
    full_outer = lax.all_gather(low_outer, "dp", axis=1, tiled=True)

    rows_pair = shared_columns(rows_in)
    b_qkv = jnp.concatenate([b_query, jnp.zeros_like(b_query), b_value])
    qkv = (mat_bf(after(rows_in, rows_pair), full_qkv) + b_qkv).astype(LOW)
    far_kv = swap(qkv[:, width_here:], "dp", 1)
    mixed, lse = attn_fwd(qkv, far_kv, own_bias[None], far_bias[None], heads_here)

    attn_parts, _, _ = scatter_rows(lambda a, b, gate: mat_bf(rows_of(gated(mixed, gate), a, b), full_out))
    resid_one, hidden, hidden_here = on_rows(
        norm_one_kernel,
        "norm_one",
        (in_here, *attn_parts, b_out[None], ln1_gain[None], ln1_bias[None]),
        (F32, F32, LOW),
        False,
    )
    hidden_low = gather_rows(hidden_here)
    inner = mat_last(hidden_low, full_inner) + b_inner
    act, act_slope = jax.jvp(gelu_tanh, (inner,), (jnp.ones_like(inner),))
    act_low, act_slope = act.astype(LOW), act_slope.astype(LOW)
    mixed_far = swap(after(mixed, hidden_low), "dp", 1)
    hidden_pair = shared_columns(after(hidden_low, act_low))
    act_far = swap(act_low, "dp", 1)
    act_low, act_slope = after((act_low, act_slope), mixed_far, act_far, hidden_pair)

    outer_parts, _, _ = scatter_rows(lambda a, b, gate: mat_bf(rows_of(gated(act_low, gate), a, b), full_outer))
    grad_two, outer_here, output, sums_two = on_rows(
        norm_two_kernel,
        "norm_two",
        (
            hidden,
            *outer_parts,
            b_outer[None],
            ln2_gain[None],
            ln2_bias[None],
            grad_out,
            live_wide,
        ),
        (F32, LOW, LOW),
        True,
    )
    near = 3 * block
    outer_near = gather_near(outer_here)

    def act_grad(rows, first):
        slope = act_slope[first * block : first * block + rows.shape[0]]
        return (mat_last(rows, full_outer) * slope.astype(F32)).astype(LOW)

    inner_here = act_grad(outer_here, 0)
    outer_near = after(outer_near, inner_here)
    outer_rest = gather_rest(outer_here, outer_near)
    near_mine, near_far = shared_columns(jnp.concatenate([outer_here, *outer_near]))
    grad_near = weight_grad([(near_mine, act_low[:near]), (near_far, act_far[:near])])
    outer_rest = after(outer_rest, grad_near)
    output_near = gather_near(after(output, *outer_rest))
    outer_rest = jnp.concatenate(outer_rest)
    rest_mine, rest_far = shared_columns(outer_rest)
    grad_w_outer = (
        grad_near + weight_grad([(rest_mine, act_low[near:]), (rest_far, act_far[near:])])
    ).astype(LOW)
    owner_outer = to_owner(grad_w_outer)
    away_rows = jnp.concatenate([*outer_near, after(outer_rest, grad_w_outer)])
    inner_away = act_grad(away_rows, 1)
    inner_low = jnp.concatenate([inner_here, inner_away])
    inner_far = swap(inner_low, "dp", 1)

    inner_three, output_near = lax.optimization_barrier(
        (mat_bf(rows_of(inner_away, 2, 3), full_inner), output_near)
    )

    def inner_part(first, last, gate):
        if first == 3:
            return inner_three
        if first == 0:
            return mat_bf(gated(inner_here, gate), full_inner)
        return mat_bf(rows_of(gated(inner_away, gate), first - 1, last - 1), full_inner)

    def inner_weight(sent):
        mine, far = after((inner_low, inner_far), sent)
        return weight_grad([(hidden_pair[0], mine), (hidden_pair[1], far)]).astype(LOW)

    hidden_parts, _, (grad_w_inner,) = scatter_rows(inner_part, (), [inner_weight])
    grad_one, attn_here, sums_one = on_rows(
        norm_one_back_kernel,
        "norm_one_back",
        (resid_one, grad_two, *hidden_parts, ln1_gain[None]),
        (F32, LOW),
        True,
    )
    owner_inner = to_owner(after(grad_w_inner, owner_outer, attn_here))
    output_rest = gather_rest(output, after(output_near, *hidden_parts))
    attn_low = gather_rows(after(attn_here, output_rest))
    mixed_low = mat_last(attn_low, full_out).astype(LOW)
    query_low, own_key, own_value, far_pair = attn_bwd(
        qkv, far_kv, mixed_low, mixed, lse, own_bias_wide, far_bias_wide, heads_here, 512, 256
    )
    attn_pair = shared_columns(after(attn_low, query_low))
    far_key, far_value = after(swap(far_pair, "dp", 1), attn_pair).astype(F32)
    key_low = (own_key + far_key).astype(LOW)
    value_low = (own_value + far_value).astype(LOW)
    qkv_low = jnp.concatenate([query_low, key_low, value_low], axis=1)
    qkv_far = swap(qkv_low, "dp", 1)

    def attn_weight(sent):
        mine, far = after((qkv_low, qkv_far), sent, owner_inner)
        grad_w_qkv = weight_grad([(rows_pair[0], mine), (rows_pair[1], far)]).astype(LOW)
        attn_mine, attn_far = after(attn_pair, grad_w_qkv)
        grad_w_out = weight_grad([(attn_mine, mixed), (attn_far, mixed_far)]).astype(LOW)
        return jnp.concatenate([grad_w_qkv, grad_w_out], axis=1)

    def total_sums(sent):
        rows = jnp.concatenate([sums_one[:3], sums_two[:3]]).reshape(-1)
        inner_sum = jnp.sum(inner_low.astype(F32), axis=0)
        qkv_sum = jnp.sum(qkv_low.astype(F32), axis=0)
        return everyone(after(jnp.concatenate([rows, inner_sum, qkv_sum]), sent), ("dp",))

    def owned(sent):
        outer, inner = after((owner_outer, owner_inner), sent)
        return outer.T.astype(F32), inner.astype(F32)

    (here, one, two), (grad_w_attn,), (sums, (grad_w_outer, grad_w_inner)) = scatter_rows(
        lambda a, b, gate: mat_last(rows_of(gated(qkv_low, gate), a, b), full_qkv),
        after_first=[attn_weight],
        after_second=[total_sums, owned],
    )
    owner_attn = to_owner(after(grad_w_attn, owner_inner))
    tokens_here = (grad_one + (here + one.astype(F32) + two.astype(F32))).astype(LOW)
    tokens_near = gather_near(tokens_here)
    output = jnp.concatenate(after((output, *output_near, *output_rest), tokens_near))
    tokens_rest = gather_rest(tokens_here, tokens_near)
    grad_tokens = jnp.concatenate([tokens_here, *tokens_near, *tokens_rest])
    output, grad_tokens = (reorder(rows).astype(F32) for rows in (output, grad_tokens))

    grad_b_inner = sums[6 * model : -3 * width_here]
    grad_b_qkv = sums[-3 * width_here :]
    sums = everyone(after(sums[: 6 * model], tokens_rest), ("tensor",)).reshape(6, model)
    grad_b_out, grad_ln1_gain, grad_ln1_bias, grad_b_outer, grad_ln2_gain, grad_ln2_bias = sums

    grad_w_attn = owner_attn.astype(F32)
    grad_w_query, grad_w_key, grad_w_value, grad_w_out = jnp.split(grad_w_attn, 4, axis=1)
    return (
        output,
        grad_tokens,
        grad_w_query,
        grad_w_key,
        grad_w_value,
        grad_b_qkv[:width_here],
        grad_b_qkv[2 * width_here :],
        grad_w_out.T,
        grad_b_out,
        grad_ln1_gain,
        grad_ln1_bias,
        grad_w_inner,
        grad_b_inner,
        grad_w_outer,
        grad_b_outer,
        grad_ln2_gain,
        grad_ln2_bias,
    )


def solution(mesh):
    return jax.shard_map(
        on_device,
        mesh=mesh,
        in_specs=(
            P("dp", None),
            P("dp", None),
            P(),
            P(),
            P("dp", "tensor"),
            P("dp", "tensor"),
            P("dp", "tensor"),
            P("tensor"),
            P("tensor"),
            P("tensor", "dp"),
            P(),
            P(),
            P(),
            P("dp", "tensor"),
            P("tensor"),
            P("tensor", "dp"),
            P(),
            P(),
            P(),
        ),
        out_specs=(
            P("dp", None),
            P("dp", None),
            P("dp", "tensor"),
            P("dp", "tensor"),
            P("dp", "tensor"),
            P("tensor"),
            P("tensor"),
            P("tensor", "dp"),
            P(),
            P(),
            P(),
            P("dp", "tensor"),
            P("tensor"),
            P("tensor", "dp"),
            P(),
            P(),
            P(),
        ),
        check_vma=False,
    )
```

```python
import functools

import jax
import jax.numpy as jnp
from jax import lax
from jax.experimental import pallas as pl
from jax.experimental.pallas import tpu as pltpu
from jax.sharding import PartitionSpec as P

HEAD_DIM = 128
SLOT = 2048
LOG2E = 1.4426950408889634

norm_eps = 1e-12

F32 = jnp.float32
LOW = jnp.bfloat16
BOTH_LAST = (((1,), (1,)), ((), ()))
BOTH_FIRST = (((0,), (0,)), ((), ()))


def gelu_tanh(inner):
    return 0.5 * inner * (1.0 + jnp.tanh(0.7978845608 * (inner + 0.044715 * inner * inner * inner)))


def mat_bf(left, right):
    return jnp.dot(left, right, preferred_element_type=F32)


def mat_last(left, right):
    return lax.dot_general(left, right, BOTH_LAST, preferred_element_type=F32)


def mat_first(left, right):
    return lax.dot_general(left, right, BOTH_FIRST, preferred_element_type=F32)


def swap(value, axis, flip):
    count = lax.axis_size(axis)
    return lax.ppermute(value, axis, [(source, source ^ flip) for source in range(count)])


def after(value, *others):
    return lax.optimization_barrier((value, *others))[0]


def everyone(value, axes):
    for axis in axes:
        flip = 1
        while flip < lax.axis_size(axis):
            value = value + swap(value, axis, flip)
            flip *= 2
    return value


def gated(value, gate):
    return value if gate is None else after(value, gate)


def gather_near(block):
    return swap(block, "tensor", 1), swap(block, "tensor", 2)


def sent_on(near):
    one, two = near
    half = one.shape[0] // 2
    return two[:half], one[half:]


def gather_sent(sent, block, near):
    rest = [swap(sent[0], "tensor", 1), swap(sent[1], "tensor", 2)]
    count, flip = lax.axis_size("tensor"), 4
    while flip < count:
        rest.append(swap(jnp.concatenate([block, *near, *rest]), "tensor", flip))
        flip *= 2
    return rest


def gather_rest(block, near):
    return gather_sent(sent_on(near), block, near)


def gather_rows(block):
    near = gather_near(block)
    return jnp.concatenate([block, *near, *gather_rest(block, near)])


def scatter_rows(part, after_first=(), after_second=()):
    count = lax.axis_size("tensor")
    flip = count // 2
    extra = None
    while flip >= 4:
        away = part(flip, 2 * flip, None)
        split = away.shape[0]
        if extra is not None:
            away = away + extra[split:].astype(F32)
        come = swap(away.astype(LOW), "tensor", flip)
        extra = come if extra is None else extra[:split].astype(F32) + come.astype(F32)
        flip //= 2

    def piece(first, last, gate=None):
        value = part(first, last, gate)
        if extra is not None:
            block = extra.shape[0] // 4
            value = value + extra[first * block : last * block].astype(F32)
        return value

    three = piece(3, 4).astype(LOW)
    half = three.shape[0] // 2
    come_top, come_low = swap(three[:half], "tensor", 1), swap(three[half:], "tensor", 2)
    first = [make(three) for make in after_first]
    one, two = jnp.split(piece(1, 3, (three, *first)), 2)
    come_top, come_low = after((come_top, come_low), *first)
    one = jnp.concatenate([one[:half].astype(LOW), (one[half:] + come_low.astype(F32)).astype(LOW)])
    two = jnp.concatenate([(two[:half] + come_top.astype(F32)).astype(LOW), two[half:].astype(LOW)])
    from_one, from_two = swap(one, "tensor", 1), swap(two, "tensor", 2)
    here = piece(0, 1, (one, two))
    second = [make((one, two)) for make in after_second]
    from_one, from_two = after((from_one, from_two), here, *jax.tree.leaves(second))
    return (here, from_one, from_two), first, second


def normed(resid):
    center = resid - jnp.mean(resid, axis=-1, keepdims=True)
    spread = jnp.mean(center * center, axis=-1, keepdims=True)
    scale = lax.rsqrt(spread + norm_eps)
    return center * scale, scale


def norm_grad(unit, scale, grad, gain):
    inner = grad * gain
    back = scale * (
        inner
        - jnp.mean(inner, axis=-1, keepdims=True)
        - unit * jnp.mean(inner * unit, axis=-1, keepdims=True)
    )
    return back, grad * unit


def add_sums(sum_ref, *terms):
    @pl.when(pl.program_id(0) == 0)
    def _():
        sum_ref[...] = jnp.zeros_like(sum_ref)

    for row, term in enumerate(terms):
        sum_ref[row : row + 1, :] += jnp.sum(term, axis=0, keepdims=True)


def received(here_ref, one_ref, two_ref):
    return here_ref[...] + one_ref[...].astype(F32) + two_ref[...].astype(F32)


def norm_one_kernel(
    in_ref, h, one, two, b_ref, gain_ref, shift_ref, resid_ref, hidden_ref, low_ref
):
    resid = in_ref[...].astype(F32) + (received(h, one, two) + b_ref[...])
    unit, _ = normed(resid)
    hidden = unit * gain_ref[...] + shift_ref[...]
    resid_ref[...] = resid
    hidden_ref[...] = hidden
    low_ref[...] = hidden.astype(LOW)


def norm_two_kernel(
    hidden_ref, h, one, two, b_ref, gain_ref, shift_ref, cot_ref, live_ref,
    grad_ref, low_ref, out_ref, sum_ref,
):
    unit, scale = normed(hidden_ref[...] + (received(h, one, two) + b_ref[...]))
    gain = gain_ref[...]
    out_ref[...] = (unit * gain + shift_ref[...]).astype(LOW)
    grad = cot_ref[...].astype(F32) * live_ref[:, 0:1]
    back, to_gain = norm_grad(unit, scale, grad, gain)
    grad_ref[...] = back
    low_ref[...] = back.astype(LOW)
    add_sums(sum_ref, back, to_gain, grad)


def norm_one_back_kernel(
    resid_ref, grad_ref, h, one, two, gain_ref, back_ref, low_ref, sum_ref
):
    grad = grad_ref[...] + received(h, one, two)
    unit, scale = normed(resid_ref[...])
    back, to_gain = norm_grad(unit, scale, grad, gain_ref[...])
    back_ref[...] = back
    low_ref[...] = back.astype(LOW)
    add_sums(sum_ref, back, to_gain, grad)


def on_rows(kernel, name, args, outs, sums, tile=64):
    rows, model = args[0].shape
    tile = min(tile, rows)

    def spec(shape):
        if shape[0] == 1:
            return pl.BlockSpec(shape, lambda i: (0, 0))
        return pl.BlockSpec((tile, shape[1]), lambda i: (i, 0))

    out_shape = [jax.ShapeDtypeStruct((rows, model), dtype) for dtype in outs]
    out_specs = [spec(out.shape) for out in out_shape]
    if sums:
        out_shape.append(jax.ShapeDtypeStruct((8, model), F32))
        out_specs.append(pl.BlockSpec((8, model), lambda i: (0, 0)))
    return pl.pallas_call(
        kernel,
        grid=(rows // tile,),
        in_specs=[spec(arg.shape) for arg in args],
        out_specs=out_specs,
        out_shape=out_shape,
        compiler_params=pltpu.CompilerParams(vmem_limit_bytes=32 << 20),
        cost_estimate=pl.CostEstimate(
            flops=20 * rows * model, transcendentals=rows, bytes_accessed=20 * rows * model
        ),
        name=name,
    )(*args)


def joined_weights_kernel(query_ref, key_ref, value_ref, out_ref, low_ref):
    width = query_ref.shape[1]
    for place, ref in enumerate((query_ref, key_ref, value_ref)):
        low_ref[place * width : (place + 1) * width, :] = jnp.transpose(ref[...]).astype(LOW)
    low_ref[3 * width :, :] = out_ref[...].astype(LOW)


def joined_weights(query, key, value, out):
    rows, width = query.shape
    return pl.pallas_call(
        joined_weights_kernel,
        out_shape=jax.ShapeDtypeStruct((4 * width, rows), LOW),
        compiler_params=pltpu.CompilerParams(vmem_limit_bytes=32 << 20),
        name="joined_weights",
    )(query, key, value, out)


def fwd_kernel(q_ref,ko_ref,kf_ref,vo_ref,vf_ref,bo_ref,bf_ref,o_ref,l_ref,*,scale):
    q=q_ref[...]
    so=lax.dot_general(q,ko_ref[...],BOTH_LAST,preferred_element_type=F32)*scale+bo_ref[...]
    sf=lax.dot_general(q,kf_ref[...],BOTH_LAST,preferred_element_type=F32)*scale+bf_ref[...]
    top=jnp.maximum(jnp.max(so,axis=1,keepdims=True),jnp.max(sf,axis=1,keepdims=True))
    po=jnp.exp2(so-top); pf=jnp.exp2(sf-top)
    tot=jnp.sum(po,axis=1,keepdims=True)+jnp.sum(pf,axis=1,keepdims=True)
    o=jnp.dot(po.astype(LOW),vo_ref[...],preferred_element_type=F32)+jnp.dot(pf.astype(LOW),vf_ref[...],preferred_element_type=F32)
    o_ref[...]=(o/tot).astype(LOW)
    lse=top+jnp.log2(tot)
    l_ref[0]=jnp.transpose(jnp.broadcast_to(lse,(lse.shape[0],HEAD_DIM)))[0:1,:]
def attn_fwd(qkv,kv_far,bias_own,bias_far,heads,bq=256):
    rows=qkv.shape[0]
    scale=LOG2E*HEAD_DIM**-0.5
    return pl.pallas_call(
        functools.partial(fwd_kernel,scale=scale),
        grid=(heads,rows//bq),
        in_specs=[pl.BlockSpec((bq,HEAD_DIM),lambda h,i:(i,h)),
          pl.BlockSpec((rows,HEAD_DIM),lambda h,i:(0,heads+h)),
          pl.BlockSpec((rows,HEAD_DIM),lambda h,i:(0,h)),
          pl.BlockSpec((rows,HEAD_DIM),lambda h,i:(0,2*heads+h)),
          pl.BlockSpec((rows,HEAD_DIM),lambda h,i:(0,heads+h)),
          pl.BlockSpec((1,rows),lambda h,i:(0,0)),
          pl.BlockSpec((1,rows),lambda h,i:(0,0))],
        out_specs=[pl.BlockSpec((bq,HEAD_DIM),lambda h,i:(i,h)),pl.BlockSpec((1,1,bq),lambda h,i:(h,0,i))],
        out_shape=[jax.ShapeDtypeStruct((rows,heads*HEAD_DIM),LOW),jax.ShapeDtypeStruct((heads,1,rows),F32)],
        compiler_params=pltpu.CompilerParams(vmem_limit_bytes=48<<20),
        cost_estimate=pl.CostEstimate(flops=12*rows*2*rows*HEAD_DIM*heads,transcendentals=heads*rows*2*rows,bytes_accessed=heads*HEAD_DIM*rows*2*6),
        name='attention_forward')(qkv,qkv,kv_far,qkv,kv_far,bias_own,bias_far)

def bwd_kernel(q_ref,do_ref,o_ref,l_ref,ko_ref,kf_ref,vo_ref,vf_ref,bo_ref,bf_ref,dq_ref,dko_ref,dvo_ref,dkf_ref,
               ako,avo,akf,avf,kto,ktf,*,scale,chunk):
    i=pl.program_id(1); last=pl.num_programs(1)-1
    @pl.when(i==0)
    def _():
        kto[...]=jnp.transpose(ko_ref[...]); ktf[...]=jnp.transpose(kf_ref[...])
        for a in (ako,avo,akf,avf): a[...]=jnp.zeros_like(a)
    q=q_ref[...]; do=do_ref[...]
    lse=l_ref[0]
    delta=jnp.sum(jnp.transpose(do.astype(F32)*o_ref[...].astype(F32)),axis=0,keepdims=True)
    rows=ko_ref.shape[0]; bq=q.shape[0]
    dqt=jnp.zeros((HEAD_DIM,bq),F32)
    for k_ref,v_ref,b_ref,ak,av,kt in ((ko_ref,vo_ref,bo_ref,ako,avo,kto),(kf_ref,vf_ref,bf_ref,akf,avf,ktf)):
        for c in range(rows//chunk):
            sl=pl.ds(c*chunk,chunk)
            st=lax.dot_general(k_ref[sl,:],q,BOTH_LAST,preferred_element_type=F32)
            b=b_ref[sl,:]
            b=jnp.concatenate([b]*(bq//HEAD_DIM),axis=1)
            p=jnp.exp2(st*scale+b-lse)
            dp=lax.dot_general(v_ref[sl,:],do,BOTH_LAST,preferred_element_type=F32)
            ds=(p*(dp-delta)).astype(LOW)
            av[sl,:]+=jnp.dot(p.astype(LOW),do,preferred_element_type=F32)
            ak[sl,:]+=jnp.dot(ds,q,preferred_element_type=F32)
            dqt=dqt+jnp.dot(kt[:,sl],ds,preferred_element_type=F32)
    s=HEAD_DIM**-0.5
    dq_ref[...]=(jnp.transpose(dqt)*s).astype(LOW)
    @pl.when(i==last)
    def _():
        dko_ref[...]=ako[...]*s; dvo_ref[...]=avo[...]
        dkf_ref[0]=(akf[...]*s).astype(LOW); dkf_ref[1]=avf[...].astype(LOW)
def attn_bwd(qkv,kv_far,do,o,lse,bias_own,bias_far,heads,bq=256,chunk=512):
    rows=qkv.shape[0]
    scale=LOG2E*HEAD_DIM**-0.5
    full=lambda off: pl.BlockSpec((rows,HEAD_DIM),lambda h,i:(0,off+h))
    qb=pl.BlockSpec((bq,HEAD_DIM),lambda h,i:(i,h))
    return pl.pallas_call(
        functools.partial(bwd_kernel,scale=scale,chunk=chunk),
        grid=(heads,rows//bq),
        in_specs=[qb,qb,qb,pl.BlockSpec((1,1,bq),lambda h,i:(h,0,i)),
          full(heads),full(0),full(2*heads),full(heads),
          pl.BlockSpec((rows,HEAD_DIM),lambda h,i:(0,0)),pl.BlockSpec((rows,HEAD_DIM),lambda h,i:(0,0))],
        out_specs=[qb,full(0),full(0),pl.BlockSpec((2,rows,HEAD_DIM),lambda h,i:(0,0,h))],
        out_shape=[jax.ShapeDtypeStruct((rows,heads*HEAD_DIM),LOW)]+[jax.ShapeDtypeStruct((rows,heads*HEAD_DIM),F32)]*2+[jax.ShapeDtypeStruct((2,rows,heads*HEAD_DIM),LOW)],
        scratch_shapes=[pltpu.VMEM((rows,HEAD_DIM),F32)]*4+[pltpu.VMEM((HEAD_DIM,rows),LOW)]*2,
        compiler_params=pltpu.CompilerParams(vmem_limit_bytes=48<<20),
        cost_estimate=pl.CostEstimate(flops=rows*heads,transcendentals=0,bytes_accessed=heads*HEAD_DIM*rows*2),
        name='attention_backward')(qkv,do,o,lse,qkv,kv_far,qkv,kv_far,bias_own,bias_far)


def on_device(
    tokens,
    cotangent,
    seq_lengths,
    slot_seq,
    w_query,
    w_key,
    w_value,
    b_query,
    b_value,
    w_out,
    b_out,
    ln1_gain,
    ln1_bias,
    w_inner,
    b_inner,
    w_outer,
    b_outer,
    ln2_gain,
    ln2_bias,
):
    tok_rows, model = tokens.shape
    assert SLOT == 2 * tok_rows
    tensor_count = lax.axis_size("tensor")
    tensor_place = lax.axis_index("tensor")
    block = tok_rows // tensor_count
    width_here = w_query.shape[1]
    heads_here = width_here // HEAD_DIM
    dp_place = lax.axis_index("dp")
    my_slot = dp_place // 2
    my_spot = dp_place % 2
    slot_ids = jnp.arange(slot_seq.shape[0])
    slot_lengths = jnp.sum(
        jnp.where(slot_seq[:, None] == slot_ids[None, :], seq_lengths[None, :], 0), axis=1
    )
    my_length = jnp.sum(jnp.where(slot_ids == my_slot, slot_lengths, 0))
    row_ids = jnp.arange(tok_rows)
    place = ((row_ids // block) ^ tensor_place) * block + row_ids % block
    own_bias = jnp.where(my_spot * tok_rows + place < my_length, 0.0, -1e30).astype(F32)
    far_bias = jnp.where((1 - my_spot) * tok_rows + place < my_length, 0.0, -1e30).astype(F32)
    own_bias_wide = jnp.broadcast_to(own_bias[:, None], (tok_rows, HEAD_DIM))
    far_bias_wide = jnp.broadcast_to(far_bias[:, None], (tok_rows, HEAD_DIM))

    def my_block(value):
        return lax.dynamic_slice_in_dim(value, tensor_place * block, block, 0)

    def reorder(value):
        return jnp.concatenate(
            [
                lax.dynamic_slice_in_dim(value, (tensor_place ^ k) * block, block, 0)
                for k in range(tensor_count)
            ]
        )

    row_live = (my_spot * tok_rows + place[:block] < my_length).astype(F32)
    rows_in = reorder(tokens)
    in_here = my_block(tokens)
    grad_out = my_block(cotangent)
    live_wide = jnp.broadcast_to(row_live[:, None], (block, HEAD_DIM))

    dp_count = lax.axis_size("dp")
    column = model // dp_count

    def columns_of(value, core):
        return jnp.concatenate(
            [
                jnp.where(
                    core == 0,
                    value[:, first : first + column],
                    value[:, first + column : first + 2 * column],
                )
                for first in range(0, model, 2 * column)
            ],
            axis=1,
        )

    def shared_columns(value):
        return columns_of(value, my_spot), swap(columns_of(value, 1 - my_spot), "dp", 1)

    def weight_grad(pairs):
        total = None
        for left, right in pairs:
            term = mat_first(left, right)
            total = term if total is None else total + term
        return total

    core_groups = [[core + 2 * step for step in range(dp_count // 2)] for core in range(2)]

    def to_owner(grad):
        return lax.psum_scatter(
            grad, "dp", scatter_dimension=0, tiled=True, axis_index_groups=core_groups
        )

    def rows_of(value, first, last):
        return value[first * block : last * block]

    low_attn = joined_weights(w_query, w_key, w_value, w_out)
    low_inner = w_inner.T.astype(LOW)
    low_outer = w_outer.astype(LOW)
    full_attn = lax.all_gather(low_attn, "dp", axis=1, tiled=True)
    full_qkv, full_out = full_attn[: 3 * width_here], full_attn[3 * width_here :]
    full_inner = lax.all_gather(low_inner, "dp", axis=1, tiled=True)
    full_outer = lax.all_gather(low_outer, "dp", axis=1, tiled=True)

    rows_pair = shared_columns(rows_in)
    b_qkv = jnp.concatenate([b_query, jnp.zeros_like(b_query), b_value])
    qkv = (mat_last(after(rows_in, rows_pair), full_qkv) + b_qkv).astype(LOW)
    far_kv = swap(qkv[:, width_here:], "dp", 1)
    mixed, lse = attn_fwd(qkv, far_kv, own_bias[None], far_bias[None], heads_here)

    attn_parts, _, _ = scatter_rows(lambda a, b, gate: mat_bf(rows_of(gated(mixed, gate), a, b), full_out))
    resid_one, hidden, hidden_here = on_rows(
        norm_one_kernel,
        "norm_one",
        (in_here, *attn_parts, b_out[None], ln1_gain[None], ln1_bias[None]),
        (F32, F32, LOW),
        False,
    )
    hidden_low = gather_rows(hidden_here)
    inner = mat_last(hidden_low, full_inner) + b_inner
    act, act_slope = jax.jvp(gelu_tanh, (inner,), (jnp.ones_like(inner),))
    act_low, act_slope = act.astype(LOW), act_slope.astype(LOW)
    mixed_far = swap(after(mixed, hidden_low), "dp", 1)
    hidden_pair = shared_columns(after(hidden_low, act_low))
    act_far = swap(act_low, "dp", 1)
    act_low, act_slope = after((act_low, act_slope), mixed_far, act_far, hidden_pair)

    outer_parts, _, _ = scatter_rows(lambda a, b, gate: mat_bf(rows_of(gated(act_low, gate), a, b), full_outer))
    grad_two, outer_here, output, sums_two = on_rows(
        norm_two_kernel,
        "norm_two",
        (
            hidden,
            *outer_parts,
            b_outer[None],
            ln2_gain[None],
            ln2_bias[None],
            grad_out,
            live_wide,
        ),
        (F32, LOW, LOW),
        True,
    )
    near = 3 * block
    outer_near = gather_near(outer_here)

    def act_grad(rows, first):
        slope = act_slope[first * block : first * block + rows.shape[0]]
        return (mat_last(rows, full_outer) * slope.astype(F32)).astype(LOW)

    inner_here = act_grad(outer_here, 0)
    outer_near = after(outer_near, inner_here)
    outer_rest = gather_rest(outer_here, outer_near)
    near_mine, near_far = shared_columns(jnp.concatenate([outer_here, *outer_near]))
    grad_near = weight_grad([(near_mine, act_low[:near]), (near_far, act_far[:near])])
    outer_rest = after(outer_rest, grad_near)
    output_near = gather_near(after(output, *outer_rest))
    outer_rest = jnp.concatenate(outer_rest)
    rest_mine, rest_far = shared_columns(outer_rest)
    grad_w_outer = (
        grad_near + weight_grad([(rest_mine, act_low[near:]), (rest_far, act_far[near:])])
    ).astype(LOW)
    owner_outer = to_owner(grad_w_outer)
    away_rows = jnp.concatenate([*outer_near, after(outer_rest, grad_w_outer)])
    inner_away = act_grad(away_rows, 1)
    inner_low = jnp.concatenate([inner_here, inner_away])
    inner_far = swap(inner_low, "dp", 1)

    inner_three, output_near = lax.optimization_barrier(
        (mat_bf(rows_of(inner_away, 2, 3), full_inner), output_near)
    )

    def inner_part(first, last, gate):
        if first == 3:
            return inner_three
        if first == 0:
            return mat_bf(gated(inner_here, gate), full_inner)
        return mat_bf(rows_of(gated(inner_away, gate), first - 1, last - 1), full_inner)

    def inner_weight(sent):
        mine, far = after((inner_low, inner_far), sent)
        return weight_grad([(hidden_pair[0], mine), (hidden_pair[1], far)]).astype(LOW)

    hidden_parts, (output_sent,), (grad_w_inner,) = scatter_rows(
        inner_part, [lambda sent: sent_on(after(output_near, sent))], [inner_weight]
    )
    grad_one, attn_here, sums_one = on_rows(
        norm_one_back_kernel,
        "norm_one_back",
        (resid_one, grad_two, *hidden_parts, ln1_gain[None]),
        (F32, LOW),
        True,
    )
    owner_inner = to_owner(after(grad_w_inner, owner_outer, attn_here))
    output_rest = gather_sent(after(output_sent, *hidden_parts), output, output_near)
    attn_low = gather_rows(after(attn_here, output_rest))
    mixed_low = mat_last(attn_low, full_out).astype(LOW)
    query_low, own_key, own_value, far_pair = attn_bwd(
        qkv, far_kv, mixed_low, mixed, lse, own_bias_wide, far_bias_wide, heads_here, 512, 256
    )
    attn_pair = shared_columns(after(attn_low, query_low))
    far_key, far_value = after(swap(far_pair, "dp", 1), attn_pair).astype(F32)
    key_low = (own_key + far_key).astype(LOW)
    value_low = (own_value + far_value).astype(LOW)
    qkv_low = jnp.concatenate([query_low, key_low, value_low], axis=1)
    qkv_far = swap(qkv_low, "dp", 1)

    def attn_weight(sent):
        mine, far = after((qkv_low, qkv_far), sent, owner_inner)
        grad_w_qkv = weight_grad([(rows_pair[0], mine), (rows_pair[1], far)]).astype(LOW)
        attn_mine, attn_far = after(attn_pair, grad_w_qkv)
        grad_w_out = weight_grad([(attn_mine, mixed), (attn_far, mixed_far)]).astype(LOW)
        return jnp.concatenate([grad_w_qkv, grad_w_out], axis=1)

    def total_sums(sent):
        rows = jnp.concatenate([sums_one[:3], sums_two[:3]]).reshape(-1)
        inner_sum = jnp.sum(inner_low.astype(F32), axis=0)
        qkv_sum = jnp.sum(qkv_low.astype(F32), axis=0)
        return everyone(after(jnp.concatenate([rows, inner_sum, qkv_sum]), sent), ("dp",))

    def owned(sent):
        outer, inner = after((owner_outer, owner_inner), sent)
        return outer.T.astype(F32), inner.astype(F32)

    (here, one, two), (grad_w_attn,), (sums, (grad_w_outer, grad_w_inner)) = scatter_rows(
        lambda a, b, gate: mat_bf(rows_of(gated(qkv_low, gate), a, b), full_qkv),
        after_first=[attn_weight],
        after_second=[total_sums, owned],
    )
    owner_attn = to_owner(after(grad_w_attn, owner_inner))
    tokens_here = (grad_one + (here + one.astype(F32) + two.astype(F32))).astype(LOW)
    tokens_near = gather_near(tokens_here)
    output = jnp.concatenate(after((output, *output_near, *output_rest), tokens_near))
    tokens_rest = gather_rest(tokens_here, tokens_near)
    grad_tokens = jnp.concatenate([tokens_here, *tokens_near, *tokens_rest])
    output, grad_tokens = (reorder(rows).astype(F32) for rows in (output, grad_tokens))

    grad_b_inner = sums[6 * model : -3 * width_here]
    grad_b_qkv = sums[-3 * width_here :]
    sums = everyone(after(sums[: 6 * model], tokens_rest), ("tensor",)).reshape(6, model)
    grad_b_out, grad_ln1_gain, grad_ln1_bias, grad_b_outer, grad_ln2_gain, grad_ln2_bias = sums

    grad_w_attn = owner_attn.astype(F32)
    grad_w_query, grad_w_key, grad_w_value, grad_w_out = jnp.split(grad_w_attn, 4, axis=1)
    return (
        output,
        grad_tokens,
        grad_w_query,
        grad_w_key,
        grad_w_value,
        grad_b_qkv[:width_here],
        grad_b_qkv[2 * width_here :],
        grad_w_out.T,
        grad_b_out,
        grad_ln1_gain,
        grad_ln1_bias,
        grad_w_inner,
        grad_b_inner,
        grad_w_outer,
        grad_b_outer,
        grad_ln2_gain,
        grad_ln2_bias,
    )


def solution(mesh):
    return jax.shard_map(
        on_device,
        mesh=mesh,
        in_specs=(
            P("dp", None),
            P("dp", None),
            P(),
            P(),
            P("dp", "tensor"),
            P("dp", "tensor"),
            P("dp", "tensor"),
            P("tensor"),
            P("tensor"),
            P("tensor", "dp"),
            P(),
            P(),
            P(),
            P("dp", "tensor"),
            P("tensor"),
            P("tensor", "dp"),
            P(),
            P(),
            P(),
        ),
        out_specs=(
            P("dp", None),
            P("dp", None),
            P("dp", "tensor"),
            P("dp", "tensor"),
            P("dp", "tensor"),
            P("tensor"),
            P("tensor"),
            P("tensor", "dp"),
            P(),
            P(),
            P(),
            P("dp", "tensor"),
            P("tensor"),
            P("tensor", "dp"),
            P(),
            P(),
            P(),
        ),
        check_vma=False,
    )
```

```python
import functools

import jax
import jax.numpy as jnp
from jax import lax
from jax.experimental import pallas as pl
from jax.experimental.pallas import tpu as pltpu
from jax.sharding import PartitionSpec as P

HEAD_DIM = 128
SLOT = 2048
LOG2E = 1.4426950408889634

norm_eps = 1e-12

F32 = jnp.float32
LOW = jnp.bfloat16
BOTH_LAST = (((1,), (1,)), ((), ()))
BOTH_FIRST = (((0,), (0,)), ((), ()))


def gelu_tanh(inner):
    return 0.5 * inner * (1.0 + jnp.tanh(0.7978845608 * (inner + 0.044715 * inner * inner * inner)))


def mat_bf(left, right):
    return jnp.dot(left, right, preferred_element_type=F32)


def mat_last(left, right):
    return lax.dot_general(left, right, BOTH_LAST, preferred_element_type=F32)


def mat_first(left, right):
    return lax.dot_general(left, right, BOTH_FIRST, preferred_element_type=F32)


def swap(value, axis, flip):
    count = lax.axis_size(axis)
    return lax.ppermute(value, axis, [(source, source ^ flip) for source in range(count)])


def after(value, *others):
    return lax.optimization_barrier((value, *others))[0]


def everyone(value, axes):
    for axis in axes:
        flip = 1
        while flip < lax.axis_size(axis):
            value = value + swap(value, axis, flip)
            flip *= 2
    return value


def gated(value, gate):
    return value if gate is None else after(value, gate)


def gather_near(block):
    return swap(block, "tensor", 1), swap(block, "tensor", 2)


def sent_on(near):
    one, two = near
    half = one.shape[0] // 2
    return two[:half], one[half:]


def gather_sent(sent, block, near):
    rest = [swap(sent[0], "tensor", 1), swap(sent[1], "tensor", 2)]
    count, flip = lax.axis_size("tensor"), 4
    while flip < count:
        rest.append(swap(jnp.concatenate([block, *near, *rest]), "tensor", flip))
        flip *= 2
    return rest


def gather_rest(block, near):
    return gather_sent(sent_on(near), block, near)


def gather_rows(block):
    near = gather_near(block)
    return jnp.concatenate([block, *near, *gather_rest(block, near)])


def scatter_rows(part, after_first=(), after_second=()):
    count = lax.axis_size("tensor")
    flip = count // 2
    extra = None
    while flip >= 4:
        away = part(flip, 2 * flip, None)
        split = away.shape[0]
        if extra is not None:
            away = away + extra[split:].astype(F32)
        come = swap(away.astype(LOW), "tensor", flip)
        extra = come if extra is None else extra[:split].astype(F32) + come.astype(F32)
        flip //= 2

    def piece(first, last, gate=None):
        value = part(first, last, gate)
        if extra is not None:
            block = extra.shape[0] // 4
            value = value + extra[first * block : last * block].astype(F32)
        return value

    three = piece(3, 4).astype(LOW)
    half = three.shape[0] // 2
    come_top, come_low = swap(three[:half], "tensor", 1), swap(three[half:], "tensor", 2)
    first = [make(three) for make in after_first]
    one, two = jnp.split(piece(1, 3, (three, *first)), 2)
    come_top, come_low = after((come_top, come_low), *first)
    one = jnp.concatenate([one[:half].astype(LOW), (one[half:] + come_low.astype(F32)).astype(LOW)])
    two = jnp.concatenate([(two[:half] + come_top.astype(F32)).astype(LOW), two[half:].astype(LOW)])
    from_one, from_two = swap(one, "tensor", 1), swap(two, "tensor", 2)
    here = piece(0, 1, (one, two))
    second = [make((one, two)) for make in after_second]
    from_one, from_two = after((from_one, from_two), here, *jax.tree.leaves(second))
    return (here, from_one, from_two), first, second


def normed(resid):
    center = resid - jnp.mean(resid, axis=-1, keepdims=True)
    spread = jnp.mean(center * center, axis=-1, keepdims=True)
    scale = lax.rsqrt(spread + norm_eps)
    return center * scale, scale


def norm_grad(unit, scale, grad, gain):
    inner = grad * gain
    back = scale * (
        inner
        - jnp.mean(inner, axis=-1, keepdims=True)
        - unit * jnp.mean(inner * unit, axis=-1, keepdims=True)
    )
    return back, grad * unit


def add_sums(sum_ref, *terms):
    @pl.when(pl.program_id(0) == 0)
    def _():
        sum_ref[...] = jnp.zeros_like(sum_ref)

    for row, term in enumerate(terms):
        sum_ref[row : row + 1, :] += jnp.sum(term, axis=0, keepdims=True)


def received(here_ref, one_ref, two_ref):
    return here_ref[...] + one_ref[...].astype(F32) + two_ref[...].astype(F32)


def norm_one_kernel(
    in_ref, h, one, two, b_ref, gain_ref, shift_ref, resid_ref, hidden_ref, low_ref
):
    resid = in_ref[...].astype(F32) + (received(h, one, two) + b_ref[...])
    unit, _ = normed(resid)
    hidden = unit * gain_ref[...] + shift_ref[...]
    resid_ref[...] = resid
    hidden_ref[...] = hidden
    low_ref[...] = hidden.astype(LOW)


def norm_two_kernel(
    hidden_ref, h, one, two, b_ref, gain_ref, shift_ref, cot_ref, live_ref,
    grad_ref, low_ref, out_ref, sum_ref,
):
    unit, scale = normed(hidden_ref[...] + (received(h, one, two) + b_ref[...]))
    gain = gain_ref[...]
    out_ref[...] = (unit * gain + shift_ref[...]).astype(LOW)
    grad = cot_ref[...].astype(F32) * live_ref[:, 0:1]
    back, to_gain = norm_grad(unit, scale, grad, gain)
    grad_ref[...] = back
    low_ref[...] = back.astype(LOW)
    add_sums(sum_ref, back, to_gain, grad)


def norm_one_back_kernel(
    resid_ref, grad_ref, h, one, two, gain_ref, back_ref, low_ref, sum_ref
):
    grad = grad_ref[...] + received(h, one, two)
    unit, scale = normed(resid_ref[...])
    back, to_gain = norm_grad(unit, scale, grad, gain_ref[...])
    back_ref[...] = back
    low_ref[...] = back.astype(LOW)
    add_sums(sum_ref, back, to_gain, grad)


def on_rows(kernel, name, args, outs, sums, tile=128):
    rows, model = args[0].shape
    tile = min(tile, rows)

    def spec(shape):
        if shape[0] == 1:
            return pl.BlockSpec(shape, lambda i: (0, 0))
        return pl.BlockSpec((tile, shape[1]), lambda i: (i, 0))

    out_shape = [jax.ShapeDtypeStruct((rows, model), dtype) for dtype in outs]
    out_specs = [spec(out.shape) for out in out_shape]
    if sums:
        out_shape.append(jax.ShapeDtypeStruct((8, model), F32))
        out_specs.append(pl.BlockSpec((8, model), lambda i: (0, 0)))
    return pl.pallas_call(
        kernel,
        grid=(rows // tile,),
        in_specs=[spec(arg.shape) for arg in args],
        out_specs=out_specs,
        out_shape=out_shape,
        compiler_params=pltpu.CompilerParams(vmem_limit_bytes=32 << 20),
        cost_estimate=pl.CostEstimate(
            flops=20 * rows * model, transcendentals=rows, bytes_accessed=20 * rows * model
        ),
        name=name,
    )(*args)


def joined_weights_kernel(query_ref, key_ref, value_ref, out_ref, low_ref):
    width = query_ref.shape[1]
    for place, ref in enumerate((query_ref, key_ref, value_ref)):
        low_ref[place * width : (place + 1) * width, :] = jnp.transpose(ref[...]).astype(LOW)
    low_ref[3 * width :, :] = out_ref[...].astype(LOW)


def joined_weights(query, key, value, out):
    rows, width = query.shape
    return pl.pallas_call(
        joined_weights_kernel,
        out_shape=jax.ShapeDtypeStruct((4 * width, rows), LOW),
        compiler_params=pltpu.CompilerParams(vmem_limit_bytes=32 << 20),
        name="joined_weights",
    )(query, key, value, out)


def fwd_kernel(q_ref,ko_ref,kf_ref,vo_ref,vf_ref,bo_ref,bf_ref,o_ref,l_ref,*,scale):
    q=q_ref[...]
    so=lax.dot_general(q,ko_ref[...],BOTH_LAST,preferred_element_type=F32)*scale+bo_ref[...]
    sf=lax.dot_general(q,kf_ref[...],BOTH_LAST,preferred_element_type=F32)*scale+bf_ref[...]
    top=jnp.maximum(jnp.max(so,axis=1,keepdims=True),jnp.max(sf,axis=1,keepdims=True))
    po=jnp.exp2(so-top); pf=jnp.exp2(sf-top)
    tot=jnp.sum(po,axis=1,keepdims=True)+jnp.sum(pf,axis=1,keepdims=True)
    o=jnp.dot(po.astype(LOW),vo_ref[...],preferred_element_type=F32)+jnp.dot(pf.astype(LOW),vf_ref[...],preferred_element_type=F32)
    o_ref[...]=(o/tot).astype(LOW)
    lse=top+jnp.log2(tot)
    l_ref[0]=jnp.transpose(jnp.broadcast_to(lse,(lse.shape[0],HEAD_DIM)))[0:1,:]
def attn_fwd(qkv,kv_far,bias_own,bias_far,heads,bq=256):
    rows=qkv.shape[0]
    scale=LOG2E*HEAD_DIM**-0.5
    return pl.pallas_call(
        functools.partial(fwd_kernel,scale=scale),
        grid=(heads,rows//bq),
        in_specs=[pl.BlockSpec((bq,HEAD_DIM),lambda h,i:(i,h)),
          pl.BlockSpec((rows,HEAD_DIM),lambda h,i:(0,heads+h)),
          pl.BlockSpec((rows,HEAD_DIM),lambda h,i:(0,h)),
          pl.BlockSpec((rows,HEAD_DIM),lambda h,i:(0,2*heads+h)),
          pl.BlockSpec((rows,HEAD_DIM),lambda h,i:(0,heads+h)),
          pl.BlockSpec((1,rows),lambda h,i:(0,0)),
          pl.BlockSpec((1,rows),lambda h,i:(0,0))],
        out_specs=[pl.BlockSpec((bq,HEAD_DIM),lambda h,i:(i,h)),pl.BlockSpec((1,1,bq),lambda h,i:(h,0,i))],
        out_shape=[jax.ShapeDtypeStruct((rows,heads*HEAD_DIM),LOW),jax.ShapeDtypeStruct((heads,1,rows),F32)],
        compiler_params=pltpu.CompilerParams(vmem_limit_bytes=48<<20),
        cost_estimate=pl.CostEstimate(flops=12*rows*2*rows*HEAD_DIM*heads,transcendentals=heads*rows*2*rows,bytes_accessed=heads*HEAD_DIM*rows*2*6),
        name='attention_forward')(qkv,qkv,kv_far,qkv,kv_far,bias_own,bias_far)

def bwd_kernel(q_ref,do_ref,o_ref,l_ref,ko_ref,kf_ref,vo_ref,vf_ref,bo_ref,bf_ref,dq_ref,dko_ref,dvo_ref,dkf_ref,
               ako,avo,akf,avf,kto,ktf,*,scale,chunk):
    i=pl.program_id(1); last=pl.num_programs(1)-1
    @pl.when(i==0)
    def _():
        kto[...]=jnp.transpose(ko_ref[...]); ktf[...]=jnp.transpose(kf_ref[...])
        for a in (ako,avo,akf,avf): a[...]=jnp.zeros_like(a)
    q=q_ref[...]; do=do_ref[...]
    lse=l_ref[0]
    delta=jnp.sum(jnp.transpose(do.astype(F32)*o_ref[...].astype(F32)),axis=0,keepdims=True)
    rows=ko_ref.shape[0]; bq=q.shape[0]
    dqt=jnp.zeros((HEAD_DIM,bq),F32)
    for k_ref,v_ref,b_ref,ak,av,kt in ((ko_ref,vo_ref,bo_ref,ako,avo,kto),(kf_ref,vf_ref,bf_ref,akf,avf,ktf)):
        for c in range(rows//chunk):
            sl=pl.ds(c*chunk,chunk)
            st=lax.dot_general(k_ref[sl,:],q,BOTH_LAST,preferred_element_type=F32)
            b=b_ref[sl,:]
            b=jnp.concatenate([b]*(bq//HEAD_DIM),axis=1)
            p=jnp.exp2(st*scale+b-lse)
            dp=lax.dot_general(v_ref[sl,:],do,BOTH_LAST,preferred_element_type=F32)
            ds=(p*(dp-delta)).astype(LOW)
            av[sl,:]+=jnp.dot(p.astype(LOW),do,preferred_element_type=F32)
            ak[sl,:]+=jnp.dot(ds,q,preferred_element_type=F32)
            dqt=dqt+jnp.dot(kt[:,sl],ds,preferred_element_type=F32)
    s=HEAD_DIM**-0.5
    dq_ref[...]=(jnp.transpose(dqt)*s).astype(LOW)
    @pl.when(i==last)
    def _():
        dko_ref[...]=ako[...]*s; dvo_ref[...]=avo[...]
        dkf_ref[0]=(akf[...]*s).astype(LOW); dkf_ref[1]=avf[...].astype(LOW)
def attn_bwd(qkv,kv_far,do,o,lse,bias_own,bias_far,heads,bq=256,chunk=512):
    rows=qkv.shape[0]
    scale=LOG2E*HEAD_DIM**-0.5
    full=lambda off: pl.BlockSpec((rows,HEAD_DIM),lambda h,i:(0,off+h))
    qb=pl.BlockSpec((bq,HEAD_DIM),lambda h,i:(i,h))
    return pl.pallas_call(
        functools.partial(bwd_kernel,scale=scale,chunk=chunk),
        grid=(heads,rows//bq),
        in_specs=[qb,qb,qb,pl.BlockSpec((1,1,bq),lambda h,i:(h,0,i)),
          full(heads),full(0),full(2*heads),full(heads),
          pl.BlockSpec((rows,HEAD_DIM),lambda h,i:(0,0)),pl.BlockSpec((rows,HEAD_DIM),lambda h,i:(0,0))],
        out_specs=[qb,full(0),full(0),pl.BlockSpec((2,rows,HEAD_DIM),lambda h,i:(0,0,h))],
        out_shape=[jax.ShapeDtypeStruct((rows,heads*HEAD_DIM),LOW)]+[jax.ShapeDtypeStruct((rows,heads*HEAD_DIM),F32)]*2+[jax.ShapeDtypeStruct((2,rows,heads*HEAD_DIM),LOW)],
        scratch_shapes=[pltpu.VMEM((rows,HEAD_DIM),F32)]*4+[pltpu.VMEM((HEAD_DIM,rows),LOW)]*2,
        compiler_params=pltpu.CompilerParams(vmem_limit_bytes=48<<20),
        cost_estimate=pl.CostEstimate(flops=rows*heads,transcendentals=0,bytes_accessed=heads*HEAD_DIM*rows*2),
        name='attention_backward')(qkv,do,o,lse,qkv,kv_far,qkv,kv_far,bias_own,bias_far)


def on_device(
    tokens,
    cotangent,
    seq_lengths,
    slot_seq,
    w_query,
    w_key,
    w_value,
    b_query,
    b_value,
    w_out,
    b_out,
    ln1_gain,
    ln1_bias,
    w_inner,
    b_inner,
    w_outer,
    b_outer,
    ln2_gain,
    ln2_bias,
):
    tok_rows, model = tokens.shape
    assert SLOT == 2 * tok_rows
    tensor_count = lax.axis_size("tensor")
    tensor_place = lax.axis_index("tensor")
    block = tok_rows // tensor_count
    width_here = w_query.shape[1]
    heads_here = width_here // HEAD_DIM
    dp_place = lax.axis_index("dp")
    my_slot = dp_place // 2
    my_spot = dp_place % 2
    slot_ids = jnp.arange(slot_seq.shape[0])
    slot_lengths = jnp.sum(
        jnp.where(slot_seq[:, None] == slot_ids[None, :], seq_lengths[None, :], 0), axis=1
    )
    my_length = jnp.sum(jnp.where(slot_ids == my_slot, slot_lengths, 0))
    row_ids = jnp.arange(tok_rows)
    place = ((row_ids // block) ^ tensor_place) * block + row_ids % block
    own_bias = jnp.where(my_spot * tok_rows + place < my_length, 0.0, -1e30).astype(F32)
    far_bias = jnp.where((1 - my_spot) * tok_rows + place < my_length, 0.0, -1e30).astype(F32)
    own_bias_wide = jnp.broadcast_to(own_bias[:, None], (tok_rows, HEAD_DIM))
    far_bias_wide = jnp.broadcast_to(far_bias[:, None], (tok_rows, HEAD_DIM))

    def my_block(value):
        return lax.dynamic_slice_in_dim(value, tensor_place * block, block, 0)

    def reorder(value):
        return jnp.concatenate(
            [
                lax.dynamic_slice_in_dim(value, (tensor_place ^ k) * block, block, 0)
                for k in range(tensor_count)
            ]
        )

    row_live = (my_spot * tok_rows + place[:block] < my_length).astype(F32)
    rows_in = reorder(tokens)
    in_here = my_block(tokens)
    grad_out = my_block(cotangent)
    live_wide = jnp.broadcast_to(row_live[:, None], (block, HEAD_DIM))

    dp_count = lax.axis_size("dp")
    column = model // dp_count

    def columns_of(value, core):
        return jnp.concatenate(
            [
                jnp.where(
                    core == 0,
                    value[:, first : first + column],
                    value[:, first + column : first + 2 * column],
                )
                for first in range(0, model, 2 * column)
            ],
            axis=1,
        )

    def shared_columns(value):
        return columns_of(value, my_spot), swap(columns_of(value, 1 - my_spot), "dp", 1)

    def weight_grad(pairs):
        total = None
        for left, right in pairs:
            term = mat_first(left, right)
            total = term if total is None else total + term
        return total

    core_groups = [[core + 2 * step for step in range(dp_count // 2)] for core in range(2)]

    def to_owner(grad):
        return lax.psum_scatter(
            grad, "dp", scatter_dimension=0, tiled=True, axis_index_groups=core_groups
        )

    def rows_of(value, first, last):
        return value[first * block : last * block]

    low_attn = joined_weights(w_query, w_key, w_value, w_out)
    low_inner = w_inner.T.astype(LOW)
    low_outer = w_outer.astype(LOW)
    full_attn = lax.all_gather(low_attn, "dp", axis=1, tiled=True)
    full_qkv, full_out = full_attn[: 3 * width_here], full_attn[3 * width_here :]
    full_inner = lax.all_gather(low_inner, "dp", axis=1, tiled=True)
    full_outer = lax.all_gather(low_outer, "dp", axis=1, tiled=True)

    rows_pair = shared_columns(rows_in)
    b_qkv = jnp.concatenate([b_query, jnp.zeros_like(b_query), b_value])
    qkv = (mat_last(after(rows_in, rows_pair), full_qkv) + b_qkv).astype(LOW)
    far_kv = swap(qkv[:, width_here:], "dp", 1)
    mixed, lse = attn_fwd(qkv, far_kv, own_bias[None], far_bias[None], heads_here)

    attn_parts, _, _ = scatter_rows(lambda a, b, gate: mat_bf(rows_of(gated(mixed, gate), a, b), full_out))
    resid_one, hidden, hidden_here = on_rows(
        norm_one_kernel,
        "norm_one",
        (in_here, *attn_parts, b_out[None], ln1_gain[None], ln1_bias[None]),
        (F32, F32, LOW),
        False,
    )
    hidden_low = gather_rows(hidden_here)
    inner = mat_last(hidden_low, full_inner) + b_inner
    act, act_slope = jax.jvp(gelu_tanh, (inner,), (jnp.ones_like(inner),))
    act_low, act_slope = act.astype(LOW), act_slope.astype(LOW)
    mixed_far = swap(after(mixed, hidden_low), "dp", 1)
    hidden_pair = shared_columns(after(hidden_low, act_low))
    act_far = swap(act_low, "dp", 1)
    act_low, act_slope = after((act_low, act_slope), mixed_far, act_far, hidden_pair)

    outer_parts, _, _ = scatter_rows(lambda a, b, gate: mat_bf(rows_of(gated(act_low, gate), a, b), full_outer))
    grad_two, outer_here, output, sums_two = on_rows(
        norm_two_kernel,
        "norm_two",
        (
            hidden,
            *outer_parts,
            b_outer[None],
            ln2_gain[None],
            ln2_bias[None],
            grad_out,
            live_wide,
        ),
        (F32, LOW, LOW),
        True,
    )
    near = 3 * block
    outer_near = gather_near(outer_here)

    def act_grad(rows, first):
        slope = act_slope[first * block : first * block + rows.shape[0]]
        return (mat_last(rows, full_outer) * slope.astype(F32)).astype(LOW)

    inner_here = act_grad(outer_here, 0)
    outer_near = after(outer_near, inner_here)
    outer_rest = gather_rest(outer_here, outer_near)
    near_mine, near_far = shared_columns(jnp.concatenate([outer_here, *outer_near]))
    grad_near = weight_grad([(near_mine, act_low[:near]), (near_far, act_far[:near])])
    outer_rest = after(outer_rest, grad_near)
    output_near = gather_near(after(output, *outer_rest))
    outer_rest = jnp.concatenate(outer_rest)
    rest_mine, rest_far = shared_columns(outer_rest)
    grad_w_outer = (
        grad_near + weight_grad([(rest_mine, act_low[near:]), (rest_far, act_far[near:])])
    ).astype(LOW)
    owner_outer = to_owner(grad_w_outer)
    away_rows = jnp.concatenate([*outer_near, after(outer_rest, grad_w_outer)])
    inner_away = act_grad(away_rows, 1)
    inner_low = jnp.concatenate([inner_here, inner_away])
    inner_far = swap(inner_low, "dp", 1)

    inner_three, output_near = lax.optimization_barrier(
        (mat_bf(rows_of(inner_away, 2, 3), full_inner), output_near)
    )

    def inner_part(first, last, gate):
        if first == 3:
            return inner_three
        if first == 0:
            return mat_bf(gated(inner_here, gate), full_inner)
        return mat_bf(rows_of(gated(inner_away, gate), first - 1, last - 1), full_inner)

    def inner_weight(sent):
        mine, far = after((inner_low, inner_far), sent)
        return weight_grad([(hidden_pair[0], mine), (hidden_pair[1], far)]).astype(LOW)

    hidden_parts, (output_sent,), (grad_w_inner,) = scatter_rows(
        inner_part, [lambda sent: sent_on(after(output_near, sent))], [inner_weight]
    )
    grad_one, attn_here, sums_one = on_rows(
        norm_one_back_kernel,
        "norm_one_back",
        (resid_one, grad_two, *hidden_parts, ln1_gain[None]),
        (F32, LOW),
        True,
    )
    owner_inner = to_owner(after(grad_w_inner, owner_outer, attn_here))
    output_rest = gather_sent(after(output_sent, *hidden_parts), output, output_near)
    attn_low = gather_rows(after(attn_here, output_rest))
    mixed_low = mat_last(attn_low, full_out).astype(LOW)
    query_low, own_key, own_value, far_pair = attn_bwd(
        qkv, far_kv, mixed_low, mixed, lse, own_bias_wide, far_bias_wide, heads_here, 512, 256
    )
    attn_pair = shared_columns(after(attn_low, query_low))
    far_key, far_value = swap(far_pair, "dp", 1).astype(F32)
    key_low = (own_key + far_key).astype(LOW)
    value_low = (own_value + far_value).astype(LOW)
    qkv_low = jnp.concatenate([query_low, key_low, value_low], axis=1)
    qkv_low = after(qkv_low, attn_pair)
    qkv_far = swap(qkv_low, "dp", 1)

    def attn_weight(sent):
        mine, far = after((qkv_low, qkv_far), sent, owner_inner)
        grad_w_qkv = weight_grad([(rows_pair[0], mine), (rows_pair[1], far)]).astype(LOW)
        attn_mine, attn_far = after(attn_pair, grad_w_qkv)
        grad_w_out = weight_grad([(attn_mine, mixed), (attn_far, mixed_far)]).astype(LOW)
        return jnp.concatenate([grad_w_qkv, grad_w_out], axis=1)

    def total_sums(sent):
        rows = jnp.concatenate([sums_one[:3], sums_two[:3]]).reshape(-1)
        inner_sum = jnp.sum(inner_low.astype(F32), axis=0)
        qkv_sum = jnp.sum(qkv_low.astype(F32), axis=0)
        return everyone(after(jnp.concatenate([rows, inner_sum, qkv_sum]), sent), ("dp",))

    def owned(sent):
        outer, inner = after((owner_outer, owner_inner), sent)
        return outer.T.astype(F32), inner.astype(F32)

    (here, one, two), (grad_w_attn,), (sums, (grad_w_outer, grad_w_inner)) = scatter_rows(
        lambda a, b, gate: mat_bf(rows_of(gated(qkv_low, gate), a, b), full_qkv),
        after_first=[attn_weight],
        after_second=[total_sums, owned],
    )
    owner_attn = to_owner(after(grad_w_attn, owner_inner))
    tokens_here = (grad_one + (here + one.astype(F32) + two.astype(F32))).astype(LOW)
    tokens_near = gather_near(tokens_here)
    output = jnp.concatenate(after((output, *output_near, *output_rest), tokens_near))
    tokens_rest = gather_rest(tokens_here, tokens_near)
    grad_tokens = jnp.concatenate([tokens_here, *tokens_near, *tokens_rest])
    output, grad_tokens = (reorder(rows).astype(F32) for rows in (output, grad_tokens))

    grad_b_inner = sums[6 * model : -3 * width_here]
    grad_b_qkv = sums[-3 * width_here :]
    sums = everyone(after(sums[: 6 * model], tokens_rest), ("tensor",)).reshape(6, model)
    grad_b_out, grad_ln1_gain, grad_ln1_bias, grad_b_outer, grad_ln2_gain, grad_ln2_bias = sums

    grad_w_attn = owner_attn.astype(F32)
    grad_w_query, grad_w_key, grad_w_value, grad_w_out = jnp.split(grad_w_attn, 4, axis=1)
    return (
        output,
        grad_tokens,
        grad_w_query,
        grad_w_key,
        grad_w_value,
        grad_b_qkv[:width_here],
        grad_b_qkv[2 * width_here :],
        grad_w_out.T,
        grad_b_out,
        grad_ln1_gain,
        grad_ln1_bias,
        grad_w_inner,
        grad_b_inner,
        grad_w_outer,
        grad_b_outer,
        grad_ln2_gain,
        grad_ln2_bias,
    )


def solution(mesh):
    return jax.shard_map(
        on_device,
        mesh=mesh,
        in_specs=(
            P("dp", None),
            P("dp", None),
            P(),
            P(),
            P("dp", "tensor"),
            P("dp", "tensor"),
            P("dp", "tensor"),
            P("tensor"),
            P("tensor"),
            P("tensor", "dp"),
            P(),
            P(),
            P(),
            P("dp", "tensor"),
            P("tensor"),
            P("tensor", "dp"),
            P(),
            P(),
            P(),
        ),
        out_specs=(
            P("dp", None),
            P("dp", None),
            P("dp", "tensor"),
            P("dp", "tensor"),
            P("dp", "tensor"),
            P("tensor"),
            P("tensor"),
            P("tensor", "dp"),
            P(),
            P(),
            P(),
            P("dp", "tensor"),
            P("tensor"),
            P("tensor", "dp"),
            P(),
            P(),
            P(),
        ),
        check_vma=False,
    )
```
